256 devices in a mesh: lyr: 4 (over z_lo, core), strip: 64 (over z_hi, x, y).
Axes of the slice: x: 4, y: 4, z: 8 (z_hi: 4, z_lo: 2; z = z_hi * 2 + z_lo), core: 2. Of those that a mesh axis runs over, the one named last changes fastest.
Arguments:
- nodes: bfloat16 [4, 2, 64, 512, 512], P('lyr', None, None, 'strip'), may hold values from -6 to 6
- upstream: bfloat16 [4, 2, 64, 512, 512], P('lyr', None, None, 'strip'), may hold values from -6 to 6
- usage: int32 [4, 2, 512, 512], P('lyr', None, 'strip'), may hold values from 0 to 15
- blockage: int32 [4, 2, 2, 512, 512], P('lyr', None, None, 'strip'), may hold values 0 or 1
- capacity: int32 [4, 2, 2, 512, 512], P('lyr', None, None, 'strip'), may hold values from 1 to 8
- w_src: bfloat16 [2, 128, 64], replicated, may hold values from -0.75 to 0.75
- w_dst: bfloat16 [2, 128, 64], replicated, may hold values from -0.75 to 0.75
- w_out: bfloat16 [2, 64, 128], replicated, may hold values from -0.5 to 0.5
Outputs:
- grad_nodes: bfloat16 [4, 2, 64, 512, 512], P('lyr', None, None, 'strip')
- grad_src: float32 [2, 128, 64], replicated
- grad_dst: float32 [2, 128, 64], replicated
- grad_out: float32 [2, 64, 128], replicated
The draws below stay inside these ranges and needn't reach their ends.
All inputs are finite; a program needn't handle non-finite values. No bound on the sum of `blockage` on one device may be relied on, other than what follows from the above.
Results may differ from the reference program's by a relative error of at most 0.0058.
Values may be sent and summed in bfloat16 or wider, within the bound.
No kernel may reach another device: no remote copies, remote signals or barrier semaphores. Data moves between devices by JAX's collectives and lax.ppermute only.
A program may use at most 128 MiB of HBM per device.

```python
import jax
import jax.numpy as jnp
from jax import lax

F = 64
H = 128
G = 512
PAIRS = 4


def plant(entries, own_key, smallest, largest):
    spot = [jax.random.randint(jax.random.fold_in(own_key, axis), (), 0, length) for axis, length in enumerate(entries.shape)]
    longest = entries.shape.index(max(entries.shape))
    neighbour = spot[:longest] + [(spot[longest] + 1) % entries.shape[longest]] + spot[longest + 1:]
    return entries.at[tuple(spot)].set(smallest).at[tuple(neighbour)].set(largest)


def block_scale(key, extent, shards, low, high):
    factor_of = 1.0
    for dim, blocks in shards:
        draws = jax.random.uniform(jax.random.fold_in(jax.random.fold_in(key, 6), dim), (blocks,), jnp.float32, low / len(shards), high / len(shards))
        factor_of = factor_of * jnp.repeat(jnp.exp(draws), extent[dim] // blocks).reshape((-1,) + (1,) * (len(extent) - 1 - dim))
    return factor_of


def gaussian(key, extent, scale, bound, split=(), dtype=jnp.bfloat16):
    loudness = block_scale(key, extent, split, -0.22, 0.18) if split else 1.0
    values = jax.random.normal(key, extent, jnp.float32) * scale * loudness
    return jnp.minimum(jnp.maximum(values, -bound), bound).astype(dtype)


def setup_inputs(seed: int = 0) -> dict:
    keys = jax.random.split(jax.random.key(seed), 9)
    return {
        "nodes": gaussian(keys[0], (PAIRS, 2, F, G, G), 1.0, 6.0, ((0, 4), (3, 64))),
        "upstream": gaussian(keys[1], (PAIRS, 2, F, G, G), 1.0, 6.0, ((0, 4), (3, 64))),
        "usage": plant(jax.random.randint(keys[2], (PAIRS, 2, G, G), 0, 16), jax.random.fold_in(keys[2], 1), 0, 15).astype(jnp.int32),
        "blockage": plant((jax.random.randint(keys[3], (PAIRS, 2, 2, G, G), 0, 8) < 1).astype(jnp.int32), jax.random.fold_in(keys[3], 1), 0, 1),
        "capacity": plant(jax.random.randint(keys[4], (PAIRS, 2, 2, G, G), 1, 9), jax.random.fold_in(keys[4], 1), 1, 8).astype(jnp.int32),
        "w_src": gaussian(keys[5], (2, H, F), F ** -0.5, 0.75),
        "w_dst": gaussian(keys[6], (2, H, F), F ** -0.5, 0.75),
        "w_out": gaussian(keys[7], (2, F, H), H ** -0.5, 0.5),
    }


def edge_grads(w_src, w_dst, w_out, x_u, x_v, d_u, d_v, gate):
    feat, rows, cols = x_u.shape
    count = rows * cols
    flat_u = x_u.reshape(feat, count)
    flat_v = x_v.reshape(feat, count)
    pre = jnp.dot(w_src, flat_u, preferred_element_type=jnp.float32) + jnp.dot(w_dst, flat_v, preferred_element_type=jnp.float32)
    sigma = jax.nn.sigmoid(pre)
    act = (pre * sigma).astype(jnp.bfloat16)
    slope = sigma * (1.0 + pre * (1.0 - sigma))
    diff = d_v.astype(jnp.float32) - d_u.astype(jnp.float32)
    g_msg = (gate[None] * diff).reshape(feat, count).astype(jnp.bfloat16)
    g_act = lax.dot_general(w_out, g_msg, (((0,), (0,)), ((), ())), preferred_element_type=jnp.float32)
    g_pre = (g_act * slope).astype(jnp.bfloat16)
    g_out = lax.dot_general(g_msg, act, (((1,), (1,)), ((), ())), preferred_element_type=jnp.float32)
    g_src = lax.dot_general(g_pre, flat_u, (((1,), (1,)), ((), ())), preferred_element_type=jnp.float32)
    g_dst = lax.dot_general(g_pre, flat_v, (((1,), (1,)), ((), ())), preferred_element_type=jnp.float32)
    gx_u = lax.dot_general(w_src, g_pre, (((0,), (0,)), ((), ())), preferred_element_type=jnp.float32)
    gx_v = lax.dot_general(w_dst, g_pre, (((0,), (0,)), ((), ())), preferred_element_type=jnp.float32)
    return (gx_u.reshape(feat, rows, cols), gx_v.reshape(feat, rows, cols), (g_src, g_dst, g_out))

def reference(nodes, upstream, usage, blockage, capacity, w_src, w_dst, w_out):
    damp = lax.rsqrt(1.0 + usage.astype(jnp.float32))[:, :, None]
    feats = (nodes.astype(jnp.float32) * damp).astype(jnp.bfloat16)
    gates = (1 - blockage).astype(jnp.float32) * capacity.astype(jnp.float32) * 0.25
    pairs = nodes.shape[0]
    feat = nodes.shape[2]
    side = nodes.shape[4]
    inside = (jnp.arange(side) < side - 1).astype(jnp.float32)
    accum = [[jnp.zeros((feat, side, side), jnp.float32) for j in range(2)] for p in range(pairs)]
    totals = [None, None]

    def add_weights(kind, parts):
        if totals[kind] is None:
            totals[kind] = parts
        else:
            totals[kind] = tuple((a + b for a, b in zip(totals[kind], parts)))
    for p in range(pairs):
        for j in range(2):
            x_u = feats[p, j]
            d_u = upstream[p, j]
            if (j + p) % 2 == 0:
                x_v = jnp.concatenate((x_u[:, 1:, :], jnp.zeros((feat, 1, side), jnp.bfloat16)), 1)
                d_v = jnp.concatenate((d_u[:, 1:, :], jnp.zeros((feat, 1, side), jnp.bfloat16)), 1)
                gate = gates[p, j, 0] * inside[:, None]
                gu, gv, parts = edge_grads(w_src[0], w_dst[0], w_out[0], x_u, x_v, d_u, d_v, gate)
                accum[p][j] = accum[p][j] + gu + jnp.concatenate((jnp.zeros((feat, 1, side), jnp.float32), gv[:, :-1, :]), 1)
            else:
                x_v = jnp.concatenate((x_u[:, :, 1:], jnp.zeros((feat, side, 1), jnp.bfloat16)), 2)
                d_v = jnp.concatenate((d_u[:, :, 1:], jnp.zeros((feat, side, 1), jnp.bfloat16)), 2)
                gate = gates[p, j, 0] * inside[None, :]
                gu, gv, parts = edge_grads(w_src[0], w_dst[0], w_out[0], x_u, x_v, d_u, d_v, gate)
                accum[p][j] = accum[p][j] + gu + jnp.concatenate((jnp.zeros((feat, side, 1), jnp.float32), gv[:, :, :-1]), 2)
            add_weights(0, parts)
            if j == 0:
                gu, gv, parts = edge_grads(w_src[1], w_dst[1], w_out[1], x_u, feats[p, 1], d_u, upstream[p, 1], gates[p, 0, 1])
                accum[p][0] = accum[p][0] + gu
                accum[p][1] = accum[p][1] + gv
                add_weights(1, parts)
            elif p < pairs - 1:
                x_v = jnp.swapaxes(feats[p + 1, 0], 1, 2)
                d_v = jnp.swapaxes(upstream[p + 1, 0], 1, 2)
                gu, gv, parts = edge_grads(w_src[1], w_dst[1], w_out[1], x_u, x_v, d_u, d_v, gates[p, 1, 1])
                accum[p][1] = accum[p][1] + gu
                accum[p + 1][0] = accum[p + 1][0] + jnp.swapaxes(gv, 1, 2)
                add_weights(1, parts)
    node_sum = jnp.stack([jnp.stack(accum[p]) for p in range(pairs)])
    grad_nodes = (upstream.astype(jnp.float32) + damp * node_sum).astype(jnp.bfloat16)
    scale = 1.0 / jnp.sqrt(jnp.float32(2 * pairs * side * side))
    grad_src = jnp.stack((totals[0][0], totals[1][0])) * scale
    grad_dst = jnp.stack((totals[0][1], totals[1][1])) * scale
    grad_out = jnp.stack((totals[0][2], totals[1][2])) * scale
    return (grad_nodes, grad_src, grad_dst, grad_out)
```

```python
import functools
import math

import jax
import jax.numpy as jnp
from jax import lax
from jax.experimental import pallas as pl
from jax.experimental.pallas import tpu as pltpu
from jax.sharding import Mesh, PartitionSpec as P


F32 = jnp.float32
BF16 = jnp.bfloat16
VMEM = pltpu.VMEM
SMEM_SPEC = pl.BlockSpec(memory_space=pltpu.SMEM)
VMEM_SPEC = pl.BlockSpec(memory_space=pltpu.VMEM)
PARAMS = pltpu.CompilerParams(vmem_limit_bytes=56 * 1024 * 1024)


def mm(a, b):
    return jnp.dot(a, b, preferred_element_type=F32)


def mm_nt(a, b):
    return lax.dot_general(a, b, (((1,), (1,)), ((), ())), preferred_element_type=F32)


def load_weights(w_src_ref, w_dst_ref, w_out_ref, t):
    w_cat = jnp.concatenate((w_src_ref[t].astype(F32), w_dst_ref[t].astype(F32)), 1)
    w_out_t = w_out_ref[t].astype(F32).T
    return w_cat.astype(BF16), w_cat.T.astype(BF16), w_out_t.astype(BF16)


def edges(weights, x_uv, diff, gate):
    w_cat, w_cat_t, w_out_t = weights
    pre = mm(w_cat, x_uv)
    sigma = 0.5 * jnp.tanh(0.5 * pre) + 0.5
    act = pre * sigma
    slope = sigma + act * (1.0 - sigma)
    g_msg = (gate * diff).astype(BF16)
    g_pre = (mm(w_out_t, g_msg) * slope).astype(BF16)
    g_w = mm_nt(g_pre, x_uv)
    g_o = mm_nt(g_msg, act.astype(BF16))
    g_x = mm(w_cat_t, g_pre)
    return g_x, g_w, g_o


def gate_of(blockage, capacity):
    return (1 - blockage).astype(F32) * capacity.astype(F32) * 0.25


def prepare_kernel(at_ref, nodes_ref, upstream_ref, usage_ref, block_ref, cap_ref,
                   xd_ref, v0_ref, v1_ref, v2_ref, v3_ref, s_ref, rim_ref,
                   xs, ds, gs):
    pair, z, xy = at_ref[0], at_ref[1], at_ref[2]
    feat, rows, cols = nodes_ref.shape[2:]
    zs = len((v0_ref, v1_ref, v2_ref, v3_ref))
    wide = cols // zs
    for j in range(2):
        damp = lax.rsqrt(1.0 + usage_ref[0, j].astype(F32))[None]
        scaled = (nodes_ref[0, j].astype(F32) * damp).reshape(feat * rows, cols)
        given = upstream_ref[0, j].astype(F32).reshape(feat * rows, cols)
        for q in range(zs):
            xs[q] = scaled[:, q * wide:(q + 1) * wide]
            ds[q] = given[:, q * wide:(q + 1) * wide]

        def row_of(r):
            at = pl.ds(r, feat, stride=rows)
            return jnp.concatenate(
                [jnp.concatenate((xs[q, at, :], ds[q, at, :]), 0) for q in range(zs)], 1
            )

        if j == 0:
            @pl.loop(0, rows)
            def _(r):
                xd_ref[0, r] = row_of(r).astype(BF16)
                for d, v_ref in enumerate((v0_ref, v1_ref, v2_ref, v3_ref)):
                    at = pl.multiple_of(lax.rem(z + d, zs) * wide, wide)
                    v_ref[r] = xd_ref[0, r, :, pl.ds(at, wide)]
        else:
            @pl.loop(0, rows // 2)
            def _(half):
                pieces = []
                for k in range(2):
                    r = half * 2 + k
                    full = row_of(r)
                    xd_ref[1, r] = full.astype(BF16)
                    pieces.append([
                        full[:, q * wide:(q + 1) * wide].T.reshape(wide // 8, 8, 2 * feat)
                        for q in range(zs)
                    ])
                for q in range(zs):
                    both = jnp.concatenate((pieces[0][q], pieces[1][q]), 1)
                    at = pl.multiple_of(q * 8 * rows + half * 16, 16)
                    s_ref[:, pl.ds(at, 16), :] = both.astype(BF16)
    present = (pair < 3).astype(F32)
    gs[...] = jnp.zeros_like(gs)
    gs[pl.ds(pl.multiple_of(xy * 8, 8), 8), :] = gate_of(block_ref[0, 1, 1], cap_ref[0, 1, 1]) * present
    turned = [
        gs[:, q * wide:(q + 1) * wide].T.reshape(wide // 8, 8, wide) for q in range(zs)
    ]
    for q in range(0, zs, 2):
        both = jnp.concatenate((turned[q], turned[q + 1]), 1)
        s_ref[:, 8 * rows * zs + q * 8:8 * rows * zs + q * 8 + 16, :] = both.astype(BF16)
    rim_ref[...] = xd_ref[lax.rem(pair, 2), 0]


def inside_kernel(at_ref, xd_ref, block_ref, cap_ref, w_src_ref, w_dst_ref, w_out_ref,
                  ns_ref, g_w_ref, g_o_ref, gates):
    pair = at_ref[0]
    feat = xd_ref.shape[2] // 2
    rows, cols = xd_ref.shape[1], xd_ref.shape[3]
    col_layer = 1 - lax.rem(pair, 2)
    planar = load_weights(w_src_ref, w_dst_ref, w_out_ref, 0)
    via = load_weights(w_src_ref, w_dst_ref, w_out_ref, 1)
    last = lax.broadcasted_iota(jnp.int32, (rows, cols), 1) < cols - 1
    gates[0] = jnp.where(last, gate_of(block_ref[0, col_layer, 0], cap_ref[0, col_layer, 0]), 0.0)
    gates[1] = gate_of(block_ref[0, 0, 1], cap_ref[0, 0, 1])
    g_w_ref[...] = jnp.zeros_like(g_w_ref)
    g_o_ref[...] = jnp.zeros_like(g_o_ref)

    @pl.loop(0, rows)
    def _(r):
        low, high = xd_ref[0, r], xd_ref[1, r]
        x_uv = jnp.concatenate((low[:feat], high[:feat]), 0)
        diff = high[feat:].astype(F32) - low[feat:].astype(F32)
        g_x, g_w, g_o = edges(via, x_uv, diff, gates[1, pl.ds(r, 1), :])
        g_w_ref[1] += g_w
        g_o_ref[1] += g_o
        ns_ref[0, r] = g_x[:feat]
        ns_ref[1, r] = g_x[feat:]
        own = xd_ref[col_layer, r].astype(F32)
        side = pltpu.roll(own, cols - 1, 1)
        x_uv = jnp.concatenate((own[:feat], side[:feat]), 0).astype(BF16)
        g_x, g_w, g_o = edges(planar, x_uv, side[feat:] - own[feat:], gates[0, pl.ds(r, 1), :])
        g_w_ref[0] += g_w
        g_o_ref[0] += g_o
        ns_ref[col_layer, r] += g_x[:feat] + pltpu.roll(g_x[feat:], 1, 1)


def rows_kernel(at_ref, xd_ref, rim_ref, block_ref, cap_ref, w_src_ref, w_dst_ref, w_out_ref,
                ns_ref, back_ref, g_w_ref, g_o_ref, gates, carry):
    pair, z, xy = at_ref[0], at_ref[1], at_ref[2]
    feat = xd_ref.shape[2] // 2
    rows, cols = xd_ref.shape[1], xd_ref.shape[3]
    row_layer = lax.rem(pair, 2)
    planar = load_weights(w_src_ref, w_dst_ref, w_out_ref, 0)
    row_ids = (z * 16 + xy) * rows + lax.broadcasted_iota(jnp.int32, (rows, cols), 0)
    gates[...] = jnp.where(
        row_ids < cols - 1, gate_of(block_ref[0, row_layer, 0], cap_ref[0, row_layer, 0]), 0.0
    )
    g_w_ref[...] = jnp.zeros_like(g_w_ref)
    g_o_ref[...] = jnp.zeros_like(g_o_ref)
    carry[...] = jnp.zeros_like(carry)

    @pl.loop(0, rows)
    def _(r):
        low = xd_ref[row_layer, r]
        high = jnp.where(r == rows - 1, rim_ref[...], xd_ref[row_layer, jnp.minimum(r + 1, rows - 1)])
        x_uv = jnp.concatenate((low[:feat], high[:feat]), 0)
        diff = high[feat:].astype(F32) - low[feat:].astype(F32)
        g_x, g_w, g_o = edges(planar, x_uv, diff, gates[pl.ds(r, 1), :])
        g_w_ref[...] += g_w
        g_o_ref[...] += g_o
        ns_ref[r] = carry[...] + g_x[:feat]
        carry[...] = g_x[feat:]

    back_ref[...] = carry[...].astype(BF16)


def cross_kernel(at_ref, r_ref, v0_ref, v1_ref, v2_ref, v3_ref, w_src_ref, w_dst_ref, w_out_ref,
                 gw_a_ref, go_a_ref, gw_b_ref, go_b_ref,
                 gu_ref, gv0_ref, gv1_ref, gv2_ref, gv3_ref, g_ref,
                 rf, vs, gvs, gate_rows, acc_w, acc_o):
    z = at_ref[1]
    zs = vs.shape[0]
    feat = vs.shape[2] // 2
    via = load_weights(w_src_ref, w_dst_ref, w_out_ref, 1)
    body = rf.shape[1]
    rf[...] = r_ref[:, :body, :].astype(F32)
    gate_rows[...] = jnp.sum(r_ref[:, body:, :].astype(F32), axis=0)
    for d, v_ref in enumerate((v0_ref, v1_ref, v2_ref, v3_ref)):
        vs[lax.rem(z + zs - d, zs)] = v_ref[...]
    acc_w[...] = jnp.zeros_like(acc_w)
    acc_o[...] = jnp.zeros_like(acc_o)

    @pl.loop(0, 8)
    def _(i):
        z2 = i // 4
        c2 = lax.rem(i, 4)
        us, vv, gg = [], [], []
        for zp in range(2):
            for cp in range(2):
                zt = z2 * 2 + zp
                cl = c2 * 2 + cp
                u = rf[:, pl.ds(zt * 64 + cl, 8, stride=8), :].reshape(128, 128).T
                us.append(u)
                vv.append(vs[zt, cl])
                gg.append(gate_rows[pl.ds(zt * 8 + cl, 1), :])
        u = jnp.concatenate(us, 1)
        v = jnp.concatenate(vv, 1)
        gate = jnp.concatenate(gg, 1)
        x_uv = jnp.concatenate((u[:feat].astype(BF16), v[:feat]), 0)
        g_x, g_w, g_o = edges(via, x_uv, v[feat:].astype(F32) - u[feat:], gate)
        acc_w[...] += g_w
        acc_o[...] += g_o
        turned = []
        for cp in range(2):
            lo, hi = cp * 128, (2 + cp) * 128
            gvs[z2 * 2, c2 * 2 + cp] = g_x[feat:, lo:lo + 128].astype(BF16)
            gvs[z2 * 2 + 1, c2 * 2 + cp] = g_x[feat:, hi:hi + 128].astype(BF16)
            both = jnp.concatenate((g_x[:feat, lo:lo + 128], g_x[:feat, hi:hi + 128]), 0)
            turned.append(both.T.reshape(16, 8, 128))
        at = pl.multiple_of(z2 * 64 + c2 * 16, 16)
        gu_ref[:, pl.ds(at, 16), :] = jnp.concatenate(turned, 1).astype(BF16)

    for d, gv_ref in enumerate((gv0_ref, gv1_ref, gv2_ref, gv3_ref)):
        gv_ref[...] = gvs[lax.rem(z + zs - d, zs)]
    g_ref[0:128] = gw_a_ref[0] + gw_b_ref[...]
    g_ref[128:256] = gw_a_ref[1] + acc_w[...]
    g_ref[256:320] = go_a_ref[0] + go_b_ref[...]
    g_ref[320:384] = go_a_ref[1] + acc_o[...]


def finish_kernel(at_ref, gu_ref, gv0_ref, gv1_ref, gv2_ref, gv3_ref, ns_a_ref, ns_b_ref, back_ref,
                  xd_ref, usage_ref, out_ref, guf, gvs, o0, o1, damps):
    pair, z = at_ref[0], at_ref[1]
    zs = gvs.shape[0]
    feat = xd_ref.shape[2] // 2
    rows, cols = xd_ref.shape[1], xd_ref.shape[3]
    row_layer = lax.rem(pair, 2)
    guf[...] = gu_ref[...].astype(F32)
    for d, gv_ref in enumerate((gv0_ref, gv1_ref, gv2_ref, gv3_ref)):
        gvs[lax.rem(z + d, zs)] = gv_ref[...]
    damps[...] = lax.rsqrt(1.0 + usage_ref[0].astype(F32))

    @pl.loop(0, rows)
    def _(r):
        first = (r == 0).astype(F32)
        extra = ns_b_ref[r] + back_ref[...].astype(F32) * first
        low = ns_a_ref[0, r] + jnp.where(row_layer == 0, extra, 0.0)
        high = ns_a_ref[1, r] + jnp.where(row_layer == 1, extra, 0.0)
        low = low + jnp.concatenate([gvs[q, r].astype(F32) for q in range(zs)], 1)
        parts = []
        for z2 in range(2):
            block = guf[:, pl.ds(z2 * 64 + r, 8, stride=8), :].reshape(128, 128).T
            parts += [block[:feat], block[feat:]]
        high = high + jnp.concatenate(parts, 1)
        low = xd_ref[0, r, feat:, :].astype(F32) + damps[0, pl.ds(r, 1), :] * low
        high = xd_ref[1, r, feat:, :].astype(F32) + damps[1, pl.ds(r, 1), :] * high
        spots = pl.ds(r, feat, stride=rows)
        for q in range(zs):
            o0[q, spots, :] = low[:, q * 128:(q + 1) * 128]
            o1[q, spots, :] = high[:, q * 128:(q + 1) * 128]

    for q in range(zs):
        lanes = slice(q * 128, (q + 1) * 128)
        out_ref[0, 0, :, :, lanes] = o0[q].reshape(feat, rows, 128).astype(BF16)
        out_ref[0, 1, :, :, lanes] = o1[q].reshape(feat, rows, 128).astype(BF16)


def shaped(*shape, dtype=F32):
    return jax.ShapeDtypeStruct(shape, dtype)


def call(kernel, out, scratch, *args):
    return pl.pallas_call(
        kernel,
        out_shape=out,
        in_specs=[SMEM_SPEC] + [VMEM_SPEC] * (len(args) - 1),
        out_specs=jax.tree.map(lambda _: VMEM_SPEC, out),
        scratch_shapes=scratch,
        compiler_params=PARAMS,
    )(*args)


def on_device(nodes, upstream, usage, blockage, capacity, w_src, w_dst, w_out):
    pair, z, xy = lax.axis_index("l"), lax.axis_index("z"), lax.axis_index("xy")
    n_l, n_z, n_xy = lax.axis_size("l"), lax.axis_size("z"), lax.axis_size("xy")
    at = jnp.stack((pair, z, xy)).astype(jnp.int32)
    feat, rows, cols = nodes.shape[2:]
    axes = ("l", "z", "xy")

    def ident(l, k, i):
        return (l * n_z + k) * n_xy + i

    def cross_pairs(d):
        return [
            (ident(l + 1, k, i), ident(l, (k + d) % n_z, i))
            for l in range(n_l - 1) for k in range(n_z) for i in range(n_xy)
        ]

    strips = n_z * n_xy
    up = [(l * strips + s + 1, l * strips + s) for l in range(n_l) for s in range(strips - 1)]
    down = [(b, a) for a, b in up]

    xd, v0, v1, v2, v3, sent, rim = call(
        prepare_kernel,
        (
            shaped(2, rows, 2 * feat, cols, dtype=BF16),
            *[shaped(rows, 2 * feat, cols // n_z, dtype=BF16)] * 4,
            shaped(n_xy, 288, 2 * feat, dtype=BF16),
            shaped(2 * feat, cols, dtype=BF16),
        ),
        [VMEM((n_z, feat * rows, 128), F32), VMEM((n_z, feat * rows, 128), F32), VMEM((128, cols), F32)],
        at, nodes, upstream, usage, blockage, capacity,
    )
    got_v = [lax.ppermute(v, axes, cross_pairs(d)) for d, v in enumerate((v0, v1, v2, v3))]
    got_u = lax.all_to_all(sent, "xy", 0, 0, tiled=True)
    rim = lax.ppermute(rim, axes, up)
    weights = (w_src, w_dst, w_out)
    ns_a, gw_a, go_a = call(
        inside_kernel,
        (shaped(2, rows, feat, cols), shaped(2, 128, 2 * feat), shaped(2, feat, 128)),
        [VMEM((2, rows, cols), F32)],
        at, xd, blockage, capacity, *weights,
    )
    ns_b, back, gw_b, go_b = call(
        rows_kernel,
        (
            shaped(rows, feat, cols), shaped(feat, cols, dtype=BF16),
            shaped(128, 2 * feat), shaped(feat, 128),
        ),
        [VMEM((rows, cols), F32), VMEM((feat, cols), F32)],
        at, xd, rim, blockage, capacity, *weights,
    )
    back = lax.ppermute(back, axes, down)
    gu, gv0, gv1, gv2, gv3, grads = call(
        cross_kernel,
        (
            shaped(n_xy, 128, 2 * feat, dtype=BF16),
            *[shaped(rows, feat, cols // n_z, dtype=BF16)] * 4,
            shaped(384, 128),
        ),
        [
            VMEM((n_xy, 256, 128), F32), VMEM((n_z, rows, 2 * feat, 128), BF16),
            VMEM((n_z, rows, feat, 128), BF16), VMEM((32, 128), F32),
            VMEM((128, 128), F32), VMEM((feat, 128), F32),
        ],
        at, got_u, *got_v, *weights, gw_a, go_a, gw_b, go_b,
    )
    got_gv = [
        lax.ppermute(g, axes, [(b, a) for a, b in cross_pairs(d)])
        for d, g in enumerate((gv0, gv1, gv2, gv3))
    ]
    got_gu = lax.all_to_all(gu, "xy", 0, 0, tiled=True)

    scale = 1.0 / math.sqrt(2 * n_l * cols * cols)
    part = lax.all_to_all(grads.reshape(n_xy, 24, 128), "xy", 0, 0, tiled=True)
    part = jnp.broadcast_to(jnp.sum(part, 0)[None], (16, 24, 128))
    part = lax.all_to_all(part, ("l", "z"), 0, 0, tiled=True)
    part = jnp.broadcast_to(jnp.sum(part, 0)[None] * scale, (16, 24, 128))
    total = lax.all_to_all(part, "xy", 0, 0, tiled=True).reshape(384, 128)

    grad_nodes = call(
        finish_kernel,
        shaped(1, 2, feat, rows, cols, dtype=BF16),
        [
            VMEM((n_xy, 128, 128), F32), VMEM((n_z, rows, feat, 128), BF16),
            VMEM((n_z, feat * rows, 128), F32), VMEM((n_z, feat * rows, 128), F32),
            VMEM((2, rows, cols), F32),
        ],
        at, got_gu, *got_gv, ns_a, ns_b, back, xd, usage,
    )
    both = total[:256].reshape(2, 128, 2 * feat)
    return grad_nodes, both[:, :, :feat], both[:, :, feat:], total[256:].reshape(2, feat, 128)


def solution(mesh):
    split = Mesh(mesh.devices.reshape(4, 4, 16), ("l", "z", "xy"))
    strip = ("z", "xy")
    placed = (
        P("l", None, None, strip, None),
        P("l", None, None, strip, None),
        P("l", None, strip, None),
        P("l", None, None, strip, None),
        P("l", None, None, strip, None),
        P(),
        P(),
        P(),
    )
    return jax.shard_map(
        on_device,
        mesh=split,
        in_specs=placed,
        out_specs=(P("l", None, None, strip, None), P(), P(), P()),
        check_vma=False,
    )
```

```python
import math

import jax
import jax.numpy as jnp
from jax import lax
from jax.experimental import pallas as pl
from jax.experimental.pallas import tpu as pltpu
from jax.sharding import Mesh, PartitionSpec as P


F32 = jnp.float32
BF16 = jnp.bfloat16
VMEM = pltpu.VMEM
VMEM_SPEC = pl.BlockSpec(memory_space=pltpu.VMEM)
PARAMS = pltpu.CompilerParams(vmem_limit_bytes=56 * 1024 * 1024)


def mm(a, b):
    return jnp.dot(a, b, preferred_element_type=F32)


def mm_nt(a, b):
    return lax.dot_general(a, b, (((1,), (1,)), ((), ())), preferred_element_type=F32)


def load_weights(w_src_ref, w_dst_ref, w_out_ref, t):
    w_cat_t = jnp.concatenate((w_src_ref[t].astype(F32), w_dst_ref[t].astype(F32)), 0)
    w_out_t = w_out_ref[t].astype(F32).T
    return w_cat_t.T.astype(BF16), w_cat_t.astype(BF16), w_out_t.astype(BF16)


def place():
    return lax.axis_index("l"), lax.axis_index("z"), lax.axis_index("xy")


def edges(weights, x_uv, diff, gate):
    w_cat, w_cat_t, w_out_t = weights
    pre = mm(w_cat, x_uv)
    sigma = 0.5 * jnp.tanh(0.5 * pre) + 0.5
    act = pre * sigma
    slope = sigma + act * (1.0 - sigma)
    g_msg = (gate * diff).astype(BF16)
    g_pre = (mm(w_out_t, g_msg) * slope).astype(BF16)
    g_w = mm_nt(x_uv, g_pre)
    g_o = mm_nt(g_msg, act.astype(BF16))
    g_x = mm(w_cat_t, g_pre)
    return g_x, g_w, g_o


def gate_of(blockage, capacity):
    return (1 - blockage).astype(F32) * capacity.astype(F32) * 0.25


def prepare_kernel(nodes_ref, upstream_ref, usage_ref, block_ref, cap_ref,
                   xd_ref, v0_ref, v1_ref, v2_ref, v3_ref, s_ref, rim_ref,
                   xs, ds, gs):
    pair, z, xy = place()
    feat, rows, cols = nodes_ref.shape[2:]
    zs = len((v0_ref, v1_ref, v2_ref, v3_ref))
    wide = cols // zs
    for j in range(2):
        damp = lax.rsqrt(1.0 + usage_ref[0, j].astype(F32))[None]
        scaled = (nodes_ref[0, j].astype(F32) * damp).reshape(feat * rows, cols)
        given = upstream_ref[0, j].astype(F32).reshape(feat * rows, cols)
        for q in range(zs):
            xs[q] = scaled[:, q * wide:(q + 1) * wide]
            ds[q] = given[:, q * wide:(q + 1) * wide]

        def row_of(r):
            at = pl.ds(r, feat, stride=rows)
            return jnp.concatenate(
                [jnp.concatenate((xs[q, at, :], ds[q, at, :]), 0) for q in range(zs)], 1
            )

        if j == 0:
            @pl.loop(0, rows)
            def _(r):
                xd_ref[0, r] = row_of(r).astype(BF16)
                for d, v_ref in enumerate((v0_ref, v1_ref, v2_ref, v3_ref)):
                    at = pl.multiple_of(lax.rem(z + d, zs) * wide, wide)
                    v_ref[r] = xd_ref[0, r, :, pl.ds(at, wide)]
        else:
            @pl.loop(0, rows // 2)
            def _(half):
                pieces = []
                for k in range(2):
                    r = half * 2 + k
                    full = row_of(r)
                    xd_ref[1, r] = full.astype(BF16)
                    pieces.append([
                        full[:, q * wide:(q + 1) * wide].T.reshape(wide // 8, 8, 2 * feat)
                        for q in range(zs)
                    ])
                for q in range(zs):
                    both = jnp.concatenate((pieces[0][q], pieces[1][q]), 1)
                    at = pl.multiple_of(q * 8 * rows + half * 16, 16)
                    s_ref[:, pl.ds(at, 16), :] = both.astype(BF16)
    present = (pair < 3).astype(F32)
    gs[...] = jnp.zeros_like(gs)
    gs[pl.ds(pl.multiple_of(xy * 8, 8), 8), :] = gate_of(block_ref[0, 1, 1], cap_ref[0, 1, 1]) * present
    turned = [
        gs[:, q * wide:(q + 1) * wide].T.reshape(wide // 8, 8, wide) for q in range(zs)
    ]
    for q in range(0, zs, 2):
        both = jnp.concatenate((turned[q], turned[q + 1]), 1)
        s_ref[:, 8 * rows * zs + q * 8:8 * rows * zs + q * 8 + 16, :] = both.astype(BF16)
    rim_ref[...] = xd_ref[lax.rem(pair, 2), 0]


def inside_kernel(xd_ref, rim_ref, block_ref, cap_ref, w_src_ref, w_dst_ref, w_out_ref,
                  ns_ref, back_ref, g_w_ref, g_o_ref, gates, carry):
    pair, z, xy = place()
    feat = xd_ref.shape[2] // 2
    rows, cols = xd_ref.shape[1], xd_ref.shape[3]
    row_layer = lax.rem(pair, 2)
    col_layer = 1 - row_layer
    planar = load_weights(w_src_ref, w_dst_ref, w_out_ref, 0)
    via = load_weights(w_src_ref, w_dst_ref, w_out_ref, 1)
    last = lax.broadcasted_iota(jnp.int32, (rows, cols), 1) < cols - 1
    row_ids = (z * 16 + xy) * rows + lax.broadcasted_iota(jnp.int32, (rows, cols), 0)
    gates[0] = jnp.where(last, gate_of(block_ref[0, col_layer, 0], cap_ref[0, col_layer, 0]), 0.0)
    gates[1] = gate_of(block_ref[0, 0, 1], cap_ref[0, 0, 1])
    gates[2] = jnp.where(
        row_ids < cols - 1, gate_of(block_ref[0, row_layer, 0], cap_ref[0, row_layer, 0]), 0.0
    )
    g_w_ref[...] = jnp.zeros_like(g_w_ref)
    g_o_ref[...] = jnp.zeros_like(g_o_ref)
    carry[...] = jnp.zeros_like(carry)

    @pl.loop(0, rows)
    def _(r):
        low, high = xd_ref[0, r], xd_ref[1, r]
        x_uv = jnp.concatenate((low[:feat], high[:feat]), 0)
        diff = high[feat:].astype(F32) - low[feat:].astype(F32)
        g_x, g_w, g_o = edges(via, x_uv, diff, gates[1, pl.ds(r, 1), :])
        g_w_ref[1] += g_w
        g_o_ref[1] += g_o
        ns_ref[0, r] = g_x[:feat]
        ns_ref[1, r] = g_x[feat:]
        own = xd_ref[col_layer, r].astype(F32)
        side = pltpu.roll(own, cols - 1, 1)
        x_uv = jnp.concatenate((own[:feat], side[:feat]), 0).astype(BF16)
        g_x, g_w, g_o = edges(planar, x_uv, side[feat:] - own[feat:], gates[0, pl.ds(r, 1), :])
        g_w_ref[0] += g_w
        g_o_ref[0] += g_o
        ns_ref[col_layer, r] += g_x[:feat] + pltpu.roll(g_x[feat:], 1, 1)
        low = xd_ref[row_layer, r]
        high = jnp.where(r == rows - 1, rim_ref[...], xd_ref[row_layer, jnp.minimum(r + 1, rows - 1)])
        x_uv = jnp.concatenate((low[:feat], high[:feat]), 0)
        diff = high[feat:].astype(F32) - low[feat:].astype(F32)
        g_x, g_w, g_o = edges(planar, x_uv, diff, gates[2, pl.ds(r, 1), :])
        g_w_ref[0] += g_w
        g_o_ref[0] += g_o
        ns_ref[row_layer, r] += carry[...] + g_x[:feat]
        carry[...] = g_x[feat:]

    back_ref[...] = carry[...].astype(BF16)


def cross_kernel(r_ref, v0_ref, v1_ref, v2_ref, v3_ref, w_src_ref, w_dst_ref, w_out_ref,
                 gw_ref, go_ref,
                 gu_ref, gv0_ref, gv1_ref, gv2_ref, gv3_ref,
                 rf, vs, gvs, gate_rows, acc_w, acc_o, total):
    _, z, _ = place()
    zs = vs.shape[0]
    feat = vs.shape[2] // 2
    via = load_weights(w_src_ref, w_dst_ref, w_out_ref, 1)
    body = rf.shape[1]
    rf[...] = r_ref[:, :body, :].astype(F32)
    gate_rows[...] = jnp.sum(r_ref[:, body:, :].astype(F32), axis=0)
    for d, v_ref in enumerate((v0_ref, v1_ref, v2_ref, v3_ref)):
        vs[lax.rem(z + zs - d, zs)] = v_ref[...]
    acc_w[...] = jnp.zeros_like(acc_w)
    acc_o[...] = jnp.zeros_like(acc_o)

    @pl.loop(0, 8)
    def _(i):
        z2 = i // 4
        c2 = lax.rem(i, 4)
        us, vv, gg = [], [], []
        for zp in range(2):
            for cp in range(2):
                zt = z2 * 2 + zp
                cl = c2 * 2 + cp
                u = rf[:, pl.ds(zt * 64 + cl, 8, stride=8), :].reshape(128, 128).T
                us.append(u)
                vv.append(vs[zt, cl])
                gg.append(gate_rows[pl.ds(zt * 8 + cl, 1), :])
        u = jnp.concatenate(us, 1)
        v = jnp.concatenate(vv, 1)
        gate = jnp.concatenate(gg, 1)
        x_uv = jnp.concatenate((u[:feat].astype(BF16), v[:feat]), 0)
        g_x, g_w, g_o = edges(via, x_uv, v[feat:].astype(F32) - u[feat:], gate)
        acc_w[...] += g_w
        acc_o[...] += g_o
        turned = []
        for cp in range(2):
            lo, hi = cp * 128, (2 + cp) * 128
            gvs[z2 * 2, c2 * 2 + cp] = g_x[feat:, lo:lo + 128].astype(BF16)
            gvs[z2 * 2 + 1, c2 * 2 + cp] = g_x[feat:, hi:hi + 128].astype(BF16)
            both = jnp.concatenate((g_x[:feat, lo:lo + 128], g_x[:feat, hi:hi + 128]), 0)
            turned.append(both.T.reshape(16, 8, 128))
        at = pl.multiple_of(z2 * 64 + c2 * 16, 16)
        gu_ref[:, pl.ds(at, 16), :] = jnp.concatenate(turned, 1).astype(BF16)

    for d, gv_ref in enumerate((gv0_ref, gv1_ref, gv2_ref, gv3_ref)):
        gv_ref[...] = gvs[lax.rem(z + zs - d, zs)]
    total[0:64] = gw_ref[0, :feat]
    total[64:128] = gw_ref[1, :feat] + acc_w[:feat]
    total[128:192] = gw_ref[0, feat:]
    total[192:256] = gw_ref[1, feat:] + acc_w[feat:]
    total[256:320] = go_ref[0]
    total[320:384] = go_ref[1] + acc_o[...]
    for k in range(16):
        piece = total[k * 24:k * 24 + 24]
        coarse = piece.astype(BF16).astype(F32)
        both = jnp.concatenate((coarse, piece - coarse), 0)
        gu_ref[k, 128:176, :] = both.astype(BF16)


def finish_kernel(gu_ref, gv0_ref, gv1_ref, gv2_ref, gv3_ref, ns_ref, back_ref,
                  xd_ref, usage_ref, out_ref, guf, gvs, o0, o1, damps):
    pair, z, _ = place()
    zs = gvs.shape[0]
    feat = xd_ref.shape[2] // 2
    rows, cols = xd_ref.shape[1], xd_ref.shape[3]
    row_layer = lax.rem(pair, 2)
    guf[...] = gu_ref[:, :128, :].astype(F32)
    for d, gv_ref in enumerate((gv0_ref, gv1_ref, gv2_ref, gv3_ref)):
        gvs[lax.rem(z + d, zs)] = gv_ref[...]
    damps[...] = lax.rsqrt(1.0 + usage_ref[0].astype(F32))
    ns_ref[row_layer, 0] += back_ref[...].astype(F32)

    @pl.loop(0, rows)
    def _(r):
        low, high = ns_ref[0, r], ns_ref[1, r]
        low = low + jnp.concatenate([gvs[q, r].astype(F32) for q in range(zs)], 1)
        parts = []
        for z2 in range(2):
            block = guf[:, pl.ds(z2 * 64 + r, 8, stride=8), :].reshape(128, 128).T
            parts += [block[:feat], block[feat:]]
        high = high + jnp.concatenate(parts, 1)
        low = xd_ref[0, r, feat:, :].astype(F32) + damps[0, pl.ds(r, 1), :] * low
        high = xd_ref[1, r, feat:, :].astype(F32) + damps[1, pl.ds(r, 1), :] * high
        spots = pl.ds(r, feat, stride=rows)
        for q in range(zs):
            o0[q, spots, :] = low[:, q * 128:(q + 1) * 128]
            o1[q, spots, :] = high[:, q * 128:(q + 1) * 128]

    for q in range(zs):
        lanes = slice(q * 128, (q + 1) * 128)
        out_ref[0, 0, :, :, lanes] = o0[q].reshape(feat, rows, 128).astype(BF16)
        out_ref[0, 1, :, :, lanes] = o1[q].reshape(feat, rows, 128).astype(BF16)


def shaped(*shape, dtype=F32):
    return jax.ShapeDtypeStruct(shape, dtype)


def call(kernel, out, scratch, *args):
    return pl.pallas_call(
        kernel,
        out_shape=out,
        in_specs=[VMEM_SPEC] * len(args),
        out_specs=jax.tree.map(lambda _: VMEM_SPEC, out),
        scratch_shapes=scratch,
        compiler_params=PARAMS,
    )(*args)


def on_device(nodes, upstream, usage, blockage, capacity, w_src, w_dst, w_out):
    n_l, n_z, n_xy = lax.axis_size("l"), lax.axis_size("z"), lax.axis_size("xy")
    feat, rows, cols = nodes.shape[2:]
    axes = ("l", "z", "xy")

    def ident(l, k, i):
        return (l * n_z + k) * n_xy + i

    def cross_pairs(d):
        return [
            (ident(l + 1, k, i), ident(l, (k + d) % n_z, i))
            for l in range(n_l - 1) for k in range(n_z) for i in range(n_xy)
        ]

    strips = n_z * n_xy
    up = [(l * strips + s + 1, l * strips + s) for l in range(n_l) for s in range(strips - 1)]
    down = [(b, a) for a, b in up]

    xd, v0, v1, v2, v3, sent, rim = call(
        prepare_kernel,
        (
            shaped(2, rows, 2 * feat, cols, dtype=BF16),
            *[shaped(rows, 2 * feat, cols // n_z, dtype=BF16)] * 4,
            shaped(n_xy, 288, 2 * feat, dtype=BF16),
            shaped(2 * feat, cols, dtype=BF16),
        ),
        [VMEM((n_z, feat * rows, 128), F32), VMEM((n_z, feat * rows, 128), F32), VMEM((128, cols), F32)],
        nodes, upstream, usage, blockage, capacity,
    )
    got_v = [lax.ppermute(v, axes, cross_pairs(d)) for d, v in enumerate((v0, v1, v2, v3))]
    got_u = lax.all_to_all(sent, "xy", 0, 0, tiled=True)
    rim = lax.ppermute(rim, axes, up)
    weights = (jnp.swapaxes(w_src, 1, 2), jnp.swapaxes(w_dst, 1, 2), w_out)
    ns, back, g_w, g_o = call(
        inside_kernel,
        (
            shaped(2, rows, feat, cols), shaped(feat, cols, dtype=BF16),
            shaped(2, 2 * feat, 128), shaped(2, feat, 128),
        ),
        [VMEM((3, rows, cols), F32), VMEM((feat, cols), F32)],
        xd, rim, blockage, capacity, *weights,
    )
    back = lax.ppermute(back, axes, down)
    gu, gv0, gv1, gv2, gv3 = call(
        cross_kernel,
        (
            shaped(n_xy, 176, 2 * feat, dtype=BF16),
            *[shaped(rows, feat, cols // n_z, dtype=BF16)] * 4,
        ),
        [
            VMEM((n_xy, 256, 128), F32), VMEM((n_z, rows, 2 * feat, 128), BF16),
            VMEM((n_z, rows, feat, 128), BF16), VMEM((32, 128), F32),
            VMEM((2 * feat, 128), F32), VMEM((feat, 128), F32), VMEM((384, 128), F32),
        ],
        got_u, *got_v, *weights, g_w, g_o,
    )
    got_gv = [
        lax.ppermute(g, axes, [(b, a) for a, b in cross_pairs(d)])
        for d, g in enumerate((gv0, gv1, gv2, gv3))
    ]
    got_gu = lax.all_to_all(gu, "xy", 0, 0, tiled=True)

    scale = 1.0 / math.sqrt(2 * n_l * cols * cols)
    part = got_gu[:, 128:, :].astype(F32).reshape(n_xy, 2, 24, 128)
    part = jnp.sum(part, (0, 1))
    part, got_gv, back = lax.optimization_barrier((part, got_gv, back))
    part = jnp.broadcast_to(part[None], (16, 24, 128))
    part = lax.all_to_all(part, ("l", "z"), 0, 0, tiled=True)

    grad_nodes = call(
        finish_kernel,
        shaped(1, 2, feat, rows, cols, dtype=BF16),
        [
            VMEM((n_xy, 128, 128), F32), VMEM((n_z, rows, feat, 128), BF16),
            VMEM((n_z, feat * rows, 128), F32), VMEM((n_z, feat * rows, 128), F32),
            VMEM((2, rows, cols), F32),
        ],
        got_gu, *got_gv, ns, back, xd, usage,
    )
    part, grad_nodes = lax.optimization_barrier((part, grad_nodes))
    part = jnp.broadcast_to(jnp.sum(part, 0)[None] * scale, (16, 24, 128))
    total = lax.all_to_all(part, "xy", 0, 0, tiled=True).reshape(3, 2, feat, 128)
    return grad_nodes, jnp.swapaxes(total[0], 1, 2), jnp.swapaxes(total[1], 1, 2), total[2]


def solution(mesh):
    split = Mesh(mesh.devices.reshape(4, 4, 16), ("l", "z", "xy"))
    strip = ("z", "xy")
    placed = (
        P("l", None, None, strip, None),
        P("l", None, None, strip, None),
        P("l", None, strip, None),
        P("l", None, None, strip, None),
        P("l", None, None, strip, None),
        P(),
        P(),
        P(),
    )
    return jax.shard_map(
        on_device,
        mesh=split,
        in_specs=placed,
        out_specs=(P("l", None, None, strip, None), P(), P(), P()),
        check_vma=False,
    )
```

```python
import math

import jax
import jax.numpy as jnp
from jax import lax
from jax.experimental import pallas as pl
from jax.experimental.pallas import tpu as pltpu
from jax.sharding import Mesh, PartitionSpec as P


F32 = jnp.float32
BF16 = jnp.bfloat16
VMEM = pltpu.VMEM
VMEM_SPEC = pl.BlockSpec(memory_space=pltpu.VMEM)
PARAMS = pltpu.CompilerParams(vmem_limit_bytes=56 * 1024 * 1024)


def mm(a, b):
    return jnp.dot(a, b, preferred_element_type=F32)


def mm_nt(a, b):
    return lax.dot_general(a, b, (((1,), (1,)), ((), ())), preferred_element_type=F32)


def load_weights(w_src_ref, w_dst_ref, w_out_ref, t):
    w_cat_t = jnp.concatenate((w_src_ref[t].astype(F32), w_dst_ref[t].astype(F32)), 0)
    w_out_t = w_out_ref[t].astype(F32).T
    return w_cat_t.T.astype(BF16), w_cat_t.astype(BF16), w_out_t.astype(BF16)


def place():
    return lax.axis_index("l"), lax.axis_index("z"), lax.axis_index("xy")


def edges(weights, x_uv, diff, gate):
    w_cat, w_cat_t, w_out_t = weights
    pre = mm(w_cat, x_uv)
    sigma = 0.5 * jnp.tanh(0.5 * pre) + 0.5
    act = pre * sigma
    slope = sigma + act * (1.0 - sigma)
    g_msg = (gate * diff).astype(BF16)
    g_pre = (mm(w_out_t, g_msg) * slope).astype(BF16)
    g_w = mm_nt(x_uv, g_pre)
    g_o = mm_nt(g_msg, act.astype(BF16))
    g_x = mm(w_cat_t, g_pre)
    return g_x, g_w, g_o


def gate_of(blockage, capacity):
    return (1 - blockage).astype(F32) * capacity.astype(F32) * 0.25


def prepare_kernel(nodes_ref, upstream_ref, usage_ref, block_ref, cap_ref,
                   xd_ref, v0_ref, v1_ref, v2_ref, v3_ref, s_ref, rim_ref,
                   xs, ds, gs):
    pair, z, xy = place()
    feat, rows, cols = nodes_ref.shape[2:]
    zs = len((v0_ref, v1_ref, v2_ref, v3_ref))
    wide = cols // zs
    for j in range(2):
        damp = lax.rsqrt(1.0 + usage_ref[0, j].astype(F32))[None]
        scaled = (nodes_ref[0, j].astype(F32) * damp).reshape(feat * rows, cols)
        given = upstream_ref[0, j].astype(F32).reshape(feat * rows, cols)
        for q in range(zs):
            xs[q] = scaled[:, q * wide:(q + 1) * wide]
            ds[q] = given[:, q * wide:(q + 1) * wide]

        def row_of(r):
            at = pl.ds(r, feat, stride=rows)
            return jnp.concatenate(
                [jnp.concatenate((xs[q, at, :], ds[q, at, :]), 0) for q in range(zs)], 1
            )

        if j == 0:
            @pl.loop(0, rows)
            def _(r):
                xd_ref[0, r] = row_of(r).astype(BF16)
                for d, v_ref in enumerate((v0_ref, v1_ref, v2_ref, v3_ref)):
                    at = pl.multiple_of(lax.rem(z + d, zs) * wide, wide)
                    v_ref[r] = xd_ref[0, r, :, pl.ds(at, wide)]
        else:
            @pl.loop(0, rows // 2)
            def _(half):
                pieces = []
                for k in range(2):
                    r = half * 2 + k
                    full = row_of(r)
                    xd_ref[1, r] = full.astype(BF16)
                    pieces.append([
                        full[:, q * wide:(q + 1) * wide].T.reshape(wide // 8, 8, 2 * feat)
                        for q in range(zs)
                    ])
                for q in range(zs):
                    both = jnp.concatenate((pieces[0][q], pieces[1][q]), 1)
                    at = pl.multiple_of(q * 8 * rows + half * 16, 16)
                    s_ref[:, pl.ds(at, 16), :] = both.astype(BF16)
    present = (pair < 3).astype(F32)
    gs[...] = jnp.zeros_like(gs)
    gs[pl.ds(pl.multiple_of(xy * 8, 8), 8), :] = gate_of(block_ref[0, 1, 1], cap_ref[0, 1, 1]) * present
    turned = [
        gs[:, q * wide:(q + 1) * wide].T.reshape(wide // 8, 8, wide) for q in range(zs)
    ]
    for q in range(0, zs, 2):
        both = jnp.concatenate((turned[q], turned[q + 1]), 1)
        s_ref[:, 8 * rows * zs + q * 8:8 * rows * zs + q * 8 + 16, :] = both.astype(BF16)
    rim_ref[...] = xd_ref[lax.rem(pair, 2), 0]


def inside_kernel(xd_ref, rim_ref, block_ref, cap_ref, w_src_ref, w_dst_ref, w_out_ref,
                  ns_ref, back_ref, g_w_ref, g_o_ref, gates, carry):
    pair, z, xy = place()
    feat = xd_ref.shape[2] // 2
    rows, cols = xd_ref.shape[1], xd_ref.shape[3]
    row_layer = lax.rem(pair, 2)
    col_layer = 1 - row_layer
    planar = load_weights(w_src_ref, w_dst_ref, w_out_ref, 0)
    via = load_weights(w_src_ref, w_dst_ref, w_out_ref, 1)
    last = lax.broadcasted_iota(jnp.int32, (rows, cols), 1) < cols - 1
    row_ids = (z * 16 + xy) * rows + lax.broadcasted_iota(jnp.int32, (rows, cols), 0)
    gates[0] = jnp.where(last, gate_of(block_ref[0, col_layer, 0], cap_ref[0, col_layer, 0]), 0.0)
    gates[1] = gate_of(block_ref[0, 0, 1], cap_ref[0, 0, 1])
    gates[2] = jnp.where(
        row_ids < cols - 1, gate_of(block_ref[0, row_layer, 0], cap_ref[0, row_layer, 0]), 0.0
    )
    g_w_ref[...] = jnp.zeros_like(g_w_ref)
    g_o_ref[...] = jnp.zeros_like(g_o_ref)
    carry[...] = jnp.zeros_like(carry)

    @pl.loop(0, rows)
    def _(r):
        low, high = xd_ref[0, r], xd_ref[1, r]
        x_uv = jnp.concatenate((low[:feat], high[:feat]), 0)
        diff = high[feat:].astype(F32) - low[feat:].astype(F32)
        g_x, g_w, g_o = edges(via, x_uv, diff, gates[1, pl.ds(r, 1), :])
        g_w_ref[1] += g_w
        g_o_ref[1] += g_o
        ns_ref[0, r] = g_x[:feat]
        ns_ref[1, r] = g_x[feat:]
        own = xd_ref[col_layer, r].astype(F32)
        side = pltpu.roll(own, cols - 1, 1)
        x_uv = jnp.concatenate((own[:feat], side[:feat]), 0).astype(BF16)
        g_x, g_w, g_o = edges(planar, x_uv, side[feat:] - own[feat:], gates[0, pl.ds(r, 1), :])
        g_w_ref[0] += g_w
        g_o_ref[0] += g_o
        ns_ref[col_layer, r] += g_x[:feat] + pltpu.roll(g_x[feat:], 1, 1)
        low = xd_ref[row_layer, r]
        high = jnp.where(r == rows - 1, rim_ref[...], xd_ref[row_layer, jnp.minimum(r + 1, rows - 1)])
        x_uv = jnp.concatenate((low[:feat], high[:feat]), 0)
        diff = high[feat:].astype(F32) - low[feat:].astype(F32)
        g_x, g_w, g_o = edges(planar, x_uv, diff, gates[2, pl.ds(r, 1), :])
        g_w_ref[0] += g_w
        g_o_ref[0] += g_o
        ns_ref[row_layer, r] += carry[...] + g_x[:feat]
        carry[...] = g_x[feat:]

    back_ref[...] = carry[...].astype(BF16)


def cross_kernel(r_ref, v0_ref, v1_ref, v2_ref, v3_ref, w_src_ref, w_dst_ref, w_out_ref,
                 gw_ref, go_ref,
                 gu_ref, gv0_ref, gv1_ref, gv2_ref, gv3_ref,
                 rf, vs, gvs, gate_rows, acc_w, acc_o, total):
    _, z, _ = place()
    zs = vs.shape[0]
    feat = vs.shape[2] // 2
    via = load_weights(w_src_ref, w_dst_ref, w_out_ref, 1)
    body = rf.shape[1]
    rf[...] = r_ref[:, :body, :].astype(F32)
    gate_rows[...] = jnp.sum(r_ref[:, body:, :].astype(F32), axis=0)
    for d, v_ref in enumerate((v0_ref, v1_ref, v2_ref, v3_ref)):
        vs[lax.rem(z + zs - d, zs)] = v_ref[...]
    acc_w[...] = jnp.zeros_like(acc_w)
    acc_o[...] = jnp.zeros_like(acc_o)

    @pl.loop(0, 8)
    def _(i):
        z2 = i // 4
        c2 = lax.rem(i, 4)
        us, vv, gg = [], [], []
        for zp in range(2):
            for cp in range(2):
                zt = z2 * 2 + zp
                cl = c2 * 2 + cp
                u = rf[:, pl.ds(zt * 64 + cl, 8, stride=8), :].reshape(128, 128).T
                us.append(u)
                vv.append(vs[zt, cl])
                gg.append(gate_rows[pl.ds(zt * 8 + cl, 1), :])
        u = jnp.concatenate(us, 1)
        v = jnp.concatenate(vv, 1)
        gate = jnp.concatenate(gg, 1)
        x_uv = jnp.concatenate((u[:feat].astype(BF16), v[:feat]), 0)
        g_x, g_w, g_o = edges(via, x_uv, v[feat:].astype(F32) - u[feat:], gate)
        acc_w[...] += g_w
        acc_o[...] += g_o
        turned = []
        for cp in range(2):
            lo, hi = cp * 128, (2 + cp) * 128
            gvs[z2 * 2, c2 * 2 + cp] = g_x[feat:, lo:lo + 128].astype(BF16)
            gvs[z2 * 2 + 1, c2 * 2 + cp] = g_x[feat:, hi:hi + 128].astype(BF16)
            both = jnp.concatenate((g_x[:feat, lo:lo + 128], g_x[:feat, hi:hi + 128]), 0)
            turned.append(both.T.reshape(16, 8, 128))
        at = pl.multiple_of(z2 * 64 + c2 * 16, 16)
        gu_ref[:, pl.ds(at, 16), :] = jnp.concatenate(turned, 1).astype(BF16)

    for d, gv_ref in enumerate((gv0_ref, gv1_ref, gv2_ref, gv3_ref)):
        gv_ref[...] = gvs[lax.rem(z + zs - d, zs)]
    total[0:64] = gw_ref[0, :feat]
    total[64:128] = gw_ref[1, :feat] + acc_w[:feat]
    total[128:192] = gw_ref[0, feat:]
    total[192:256] = gw_ref[1, feat:] + acc_w[feat:]
    total[256:320] = go_ref[0]
    total[320:384] = go_ref[1] + acc_o[...]
    for k in range(16):
        piece = total[k * 24:k * 24 + 24]
        coarse = piece.astype(BF16).astype(F32)
        both = jnp.concatenate((coarse, piece - coarse), 0)
        gu_ref[k, 128:176, :] = both.astype(BF16)


def finish_kernel(gu_ref, gv0_ref, gv1_ref, gv2_ref, gv3_ref, ns_ref, back_ref,
                  xd_ref, usage_ref, out_ref, guf, gvs, o0, o1, damps):
    pair, z, _ = place()
    zs = gvs.shape[0]
    feat = xd_ref.shape[2] // 2
    rows = xd_ref.shape[1]
    row_layer = lax.rem(pair, 2)
    guf[...] = gu_ref[:, :128, :].astype(F32)
    for d, gv_ref in enumerate((gv0_ref, gv1_ref, gv2_ref, gv3_ref)):
        gvs[lax.rem(z + d, zs)] = gv_ref[...]
    damps[...] = lax.rsqrt(1.0 + usage_ref[0].astype(F32))
    ns_ref[row_layer, 0] += back_ref[...].astype(F32)

    @pl.loop(0, rows)
    def _(r):
        low, high = ns_ref[0, r], ns_ref[1, r]
        low = low + jnp.concatenate([gvs[q, r].astype(F32) for q in range(zs)], 1)
        parts = []
        for z2 in range(2):
            block = guf[:, pl.ds(z2 * 64 + r, 8, stride=8), :].reshape(128, 128).T
            parts += [block[:feat], block[feat:]]
        high = high + jnp.concatenate(parts, 1)
        low = xd_ref[0, r, feat:, :].astype(F32) + damps[0, pl.ds(r, 1), :] * low
        high = xd_ref[1, r, feat:, :].astype(F32) + damps[1, pl.ds(r, 1), :] * high
        spots = pl.ds(r, feat, stride=rows)
        for q in range(zs):
            o0[q, spots, :] = low[:, q * 128:(q + 1) * 128]
            o1[q, spots, :] = high[:, q * 128:(q + 1) * 128]

    for q in range(zs):
        lanes = slice(q * 128, (q + 1) * 128)
        out_ref[0, 0, :, :, lanes] = o0[q].reshape(feat, rows, 128).astype(BF16)
        out_ref[0, 1, :, :, lanes] = o1[q].reshape(feat, rows, 128).astype(BF16)


def shaped(*shape, dtype=F32):
    return jax.ShapeDtypeStruct(shape, dtype)


def all_to_all(value, axes):
    return lax.all_to_all(value, axes, 0, 0, tiled=True)


def call(kernel, out, scratch, *args):
    return pl.pallas_call(
        kernel,
        out_shape=out,
        in_specs=[VMEM_SPEC] * len(args),
        out_specs=jax.tree.map(lambda _: VMEM_SPEC, out),
        scratch_shapes=scratch,
        compiler_params=PARAMS,
    )(*args)


def on_device(nodes, upstream, usage, blockage, capacity, w_src, w_dst, w_out):
    n_l, n_z, n_xy = lax.axis_size("l"), lax.axis_size("z"), lax.axis_size("xy")
    feat, rows, cols = nodes.shape[2:]
    axes = ("l", "z", "xy")

    def ident(l, k, i):
        return (l * n_z + k) * n_xy + i

    def cross_pairs(d):
        return [
            (ident(l + 1, k, i), ident(l, (k + d) % n_z, i))
            for l in range(n_l - 1) for k in range(n_z) for i in range(n_xy)
        ]

    strips = n_z * n_xy
    up = [(l * strips + s + 1, l * strips + s) for l in range(n_l) for s in range(strips - 1)]
    down = [(b, a) for a, b in up]

    xd, v0, v1, v2, v3, sent, rim = call(
        prepare_kernel,
        (
            shaped(2, rows, 2 * feat, cols, dtype=BF16),
            *[shaped(rows, 2 * feat, cols // n_z, dtype=BF16)] * 4,
            shaped(n_xy, 288, 2 * feat, dtype=BF16),
            shaped(2 * feat, cols, dtype=BF16),
        ),
        [VMEM((n_z, feat * rows, 128), F32), VMEM((n_z, feat * rows, 128), F32), VMEM((128, cols), F32)],
        nodes, upstream, usage, blockage, capacity,
    )
    rim = lax.ppermute(rim, axes, up)
    got_u = all_to_all(sent, "xy")
    got_v = [lax.ppermute(v, axes, cross_pairs(d)) for d, v in enumerate((v0, v1, v2, v3))]
    weights = (jnp.swapaxes(w_src, 1, 2), jnp.swapaxes(w_dst, 1, 2), w_out)
    ns, back, g_w, g_o = call(
        inside_kernel,
        (
            shaped(2, rows, feat, cols), shaped(feat, cols, dtype=BF16),
            shaped(2, 2 * feat, 128), shaped(2, feat, 128),
        ),
        [VMEM((3, rows, cols), F32), VMEM((feat, cols), F32)],
        xd, rim, blockage, capacity, *weights,
    )
    back = lax.ppermute(back, axes, down)
    gu, gv0, gv1, gv2, gv3 = call(
        cross_kernel,
        (
            shaped(n_xy, 176, 2 * feat, dtype=BF16),
            *[shaped(rows, feat, cols // n_z, dtype=BF16)] * 4,
        ),
        [
            VMEM((n_xy, 256, 128), F32), VMEM((n_z, rows, 2 * feat, 128), BF16),
            VMEM((n_z, rows, feat, 128), BF16), VMEM((32, 128), F32),
            VMEM((2 * feat, 128), F32), VMEM((feat, 128), F32), VMEM((384, 128), F32),
        ],
        got_u, *got_v, *weights, g_w, g_o,
    )
    got_gu = all_to_all(gu, "xy")
    got_gv = [
        lax.ppermute(g, axes, [(b, a) for a, b in cross_pairs(d)])
        for d, g in enumerate((gv0, gv1, gv2, gv3))
    ]

    scale = 1.0 / math.sqrt(2 * n_l * cols * cols)
    part = got_gu[:, 128:, :].astype(F32).reshape(n_xy, 2, 24, 128)
    part = jnp.broadcast_to(jnp.sum(part, (0, 1))[None], (16, 24, 128))
    part = all_to_all(part, ("l", "z"))
    part, got_gv[3], back = lax.optimization_barrier((part, got_gv[3], back))

    grad_nodes = call(
        finish_kernel,
        shaped(1, 2, feat, rows, cols, dtype=BF16),
        [
            VMEM((n_xy, 128, 128), F32), VMEM((n_z, rows, feat, 128), BF16),
            VMEM((n_z, feat * rows, 128), F32), VMEM((n_z, feat * rows, 128), F32),
            VMEM((2, rows, cols), F32),
        ],
        got_gu, *got_gv, ns, back, xd, usage,
    )
    part = jnp.broadcast_to(jnp.sum(part, 0)[None] * scale, (16, 24, 128))
    total = all_to_all(part, "xy").reshape(3, 2, feat, 128)
    return grad_nodes, jnp.swapaxes(total[0], 1, 2), jnp.swapaxes(total[1], 1, 2), total[2]


def solution(mesh):
    split = Mesh(mesh.devices.reshape(4, 4, 16), ("l", "z", "xy"))
    strip = ("z", "xy")
    placed = (
        P("l", None, None, strip, None),
        P("l", None, None, strip, None),
        P("l", None, strip, None),
        P("l", None, None, strip, None),
        P("l", None, None, strip, None),
        P(),
        P(),
        P(),
    )
    return jax.shard_map(
        on_device,
        mesh=split,
        in_specs=placed,
        out_specs=(P("l", None, None, strip, None), P(), P(), P()),
        check_vma=False,
    )
```

```python
import math

import jax
import jax.numpy as jnp
from jax import lax
from jax.experimental import pallas as pl
from jax.experimental.pallas import tpu as pltpu
from jax.sharding import Mesh, PartitionSpec as P


F32 = jnp.float32
BF16 = jnp.bfloat16
VMEM = pltpu.VMEM
VMEM_SPEC = pl.BlockSpec(memory_space=pltpu.VMEM)
HBM_SPEC = pl.BlockSpec(memory_space=pltpu.HBM)
DMA = pltpu.SemaphoreType.DMA
PARAMS = pltpu.CompilerParams(vmem_limit_bytes=24 * 1024 * 1024)


def copies(sems, *pairs):
    made = [pltpu.make_async_copy(a, b, sems.at[i]) for i, (a, b) in enumerate(pairs)]
    for copy in made:
        copy.start()
    return made


def finish(made):
    for copy in made:
        copy.wait()


def mm(a, b):
    return jnp.dot(a, b, preferred_element_type=F32)


def mm_nt(a, b):
    return lax.dot_general(a, b, (((1,), (1,)), ((), ())), preferred_element_type=F32)


def load_weights(w_src_ref, w_dst_ref, w_out_ref, t):
    w_cat_t = jnp.concatenate((w_src_ref[t].astype(F32), w_dst_ref[t].astype(F32)), 0)
    w_out_t = w_out_ref[t].astype(F32).T
    return w_cat_t.T.astype(BF16), w_cat_t.astype(BF16), w_out_t.astype(BF16)


def place():
    return lax.axis_index("l"), lax.axis_index("z"), lax.axis_index("xy")


def edges(weights, x_uv, diff, gate):
    w_cat, w_cat_t, w_out_t = weights
    pre = mm(w_cat, x_uv)
    sigma = 0.5 * jnp.tanh(0.5 * pre) + 0.5
    act = pre * sigma
    slope = sigma + act * (1.0 - sigma)
    g_msg = (gate * diff).astype(BF16)
    g_pre = (mm(w_out_t, g_msg) * slope).astype(BF16)
    g_w = mm_nt(x_uv, g_pre)
    g_o = mm_nt(g_msg, act.astype(BF16))
    g_x = mm(w_cat_t, g_pre)
    return g_x, g_w, g_o


def gate_of(blockage, capacity):
    return (1 - blockage).astype(F32) * capacity.astype(F32) * 0.25


def prepare_kernel(nodes_hbm, upstream_hbm, usage_hbm, block_hbm, cap_hbm,
                   xd_hbm, v0_hbm, v1_hbm, v2_hbm, v3_hbm, s_hbm, rim_hbm,
                   xs, ds, gs, nodes_ref, upstream_ref, usage_ref, block_ref, cap_ref,
                   xd_ref, v_ref, s_ref, in_sems, out_sems):
    pair, z, xy = place()
    feat, rows, cols = nodes_ref.shape[1:]
    zs = v_ref.shape[0]
    wide = cols // zs
    loads = copies(
        in_sems,
        (usage_hbm.at[0], usage_ref),
        (nodes_hbm.at[0, 0], nodes_ref.at[0]),
        (upstream_hbm.at[0, 0], upstream_ref.at[0]),
        (nodes_hbm.at[0, 1], nodes_ref.at[1]),
        (upstream_hbm.at[0, 1], upstream_ref.at[1]),
        (block_hbm.at[0, 1, 1], block_ref),
        (cap_hbm.at[0, 1, 1], cap_ref),
    )
    stores = []
    for j in range(2):
        finish(loads[:3] if j == 0 else loads[3:])
        damp = lax.rsqrt(1.0 + usage_ref[j].astype(F32))[None]
        scaled = (nodes_ref[j].astype(F32) * damp).reshape(feat * rows, cols)
        given = upstream_ref[j].astype(F32).reshape(feat * rows, cols)
        for q in range(zs):
            xs[q] = scaled[:, q * wide:(q + 1) * wide]
            ds[q] = given[:, q * wide:(q + 1) * wide]

        def row_of(r):
            at = pl.ds(r, feat, stride=rows)
            return jnp.concatenate(
                [jnp.concatenate((xs[q, at, :], ds[q, at, :]), 0) for q in range(zs)], 1
            )

        if j == 0:
            @pl.loop(0, rows)
            def _(r):
                xd_ref[0, r] = row_of(r).astype(BF16)
                for d in range(zs):
                    at = pl.multiple_of(lax.rem(z + d, zs) * wide, wide)
                    v_ref[d, r] = xd_ref[0, r, :, pl.ds(at, wide)]

            stores += copies(
                out_sems,
                (xd_ref.at[0], xd_hbm.at[0]),
                (v_ref.at[0], v0_hbm),
                (v_ref.at[1], v1_hbm),
                (v_ref.at[2], v2_hbm),
                (v_ref.at[3], v3_hbm),
            )
        else:
            @pl.loop(0, rows // 2)
            def _(half):
                pieces = []
                for k in range(2):
                    r = half * 2 + k
                    full = row_of(r)
                    xd_ref[1, r] = full.astype(BF16)
                    pieces.append([
                        full[:, q * wide:(q + 1) * wide].T.reshape(wide // 8, 8, 2 * feat)
                        for q in range(zs)
                    ])
                for q in range(zs):
                    both = jnp.concatenate((pieces[0][q], pieces[1][q]), 1)
                    at = pl.multiple_of(q * 8 * rows + half * 16, 16)
                    s_ref[:, pl.ds(at, 16), :] = both.astype(BF16)
    present = (pair < 3).astype(F32)
    gs[...] = jnp.zeros_like(gs)
    gs[pl.ds(pl.multiple_of(xy * 8, 8), 8), :] = gate_of(block_ref[...], cap_ref[...]) * present
    turned = [
        gs[:, q * wide:(q + 1) * wide].T.reshape(wide // 8, 8, wide) for q in range(zs)
    ]
    for q in range(0, zs, 2):
        both = jnp.concatenate((turned[q], turned[q + 1]), 1)
        s_ref[:, 8 * rows * zs + q * 8:8 * rows * zs + q * 8 + 16, :] = both.astype(BF16)
    stores += copies(
        out_sems.at[5:],
        (s_ref, s_hbm),
        (xd_ref.at[lax.rem(pair, 2), 0], rim_hbm),
        (xd_ref.at[1], xd_hbm.at[1]),
    )
    finish(stores)


def inside_kernel(rim_ref, xd_hbm, block_hbm, cap_hbm, w_src_hbm, w_dst_hbm, w_out_hbm,
                  ns_hbm, back_hbm, g_w_hbm, g_o_hbm,
                  gates, carry, xd_ref, block_ref, cap_ref, w_src_ref, w_dst_ref, w_out_ref,
                  ns_ref, back_ref, g_w_ref, g_o_ref, in_sems, row_sems, ns_sems, out_sems):
    pair, z, xy = place()
    loads = copies(
        in_sems,
        (block_hbm, block_ref), (cap_hbm, cap_ref),
        (w_src_hbm, w_src_ref), (w_dst_hbm, w_dst_ref), (w_out_hbm, w_out_ref),
    )

    def row_in(r):
        return pltpu.make_async_copy(xd_hbm.at[:, r], xd_ref.at[:, r], row_sems.at[r])

    def row_out(r):
        return pltpu.make_async_copy(ns_ref.at[:, r], ns_hbm.at[:, r], ns_sems.at[r])

    for r in range(xd_ref.shape[1]):
        row_in(r).start()
    finish(loads)
    feat = xd_ref.shape[2] // 2
    rows, cols = xd_ref.shape[1], xd_ref.shape[3]
    row_layer = lax.rem(pair, 2)
    col_layer = 1 - row_layer
    planar = load_weights(w_src_ref, w_dst_ref, w_out_ref, 0)
    via = load_weights(w_src_ref, w_dst_ref, w_out_ref, 1)
    last = lax.broadcasted_iota(jnp.int32, (rows, cols), 1) < cols - 1
    row_ids = (z * 16 + xy) * rows + lax.broadcasted_iota(jnp.int32, (rows, cols), 0)
    gates[0] = jnp.where(last, gate_of(block_ref[0, col_layer, 0], cap_ref[0, col_layer, 0]), 0.0)
    gates[1] = gate_of(block_ref[0, 0, 1], cap_ref[0, 0, 1])
    gates[2] = jnp.where(
        row_ids < cols - 1, gate_of(block_ref[0, row_layer, 0], cap_ref[0, row_layer, 0]), 0.0
    )
    g_w_ref[...] = jnp.zeros_like(g_w_ref)
    g_o_ref[...] = jnp.zeros_like(g_o_ref)
    carry[...] = jnp.zeros_like(carry)
    row_in(0).wait()

    @pl.loop(0, rows, unroll=2)
    def _(r):
        @pl.when(r + 1 < rows)
        def _():
            row_in(r + 1).wait()

        low, high = xd_ref[0, r], xd_ref[1, r]
        x_uv = jnp.concatenate((low[:feat], high[:feat]), 0)
        diff = high[feat:].astype(F32) - low[feat:].astype(F32)
        g_x, g_w, g_o = edges(via, x_uv, diff, gates[1, pl.ds(r, 1), :])
        g_w_ref[1] += g_w
        g_o_ref[1] += g_o
        ns_ref[0, r] = g_x[:feat]
        ns_ref[1, r] = g_x[feat:]
        own = xd_ref[col_layer, r].astype(F32)
        side = pltpu.roll(own, cols - 1, 1)
        x_uv = jnp.concatenate((own[:feat], side[:feat]), 0).astype(BF16)
        g_x, g_w, g_o = edges(planar, x_uv, side[feat:] - own[feat:], gates[0, pl.ds(r, 1), :])
        g_w_ref[0] += g_w
        g_o_ref[0] += g_o
        ns_ref[col_layer, r] += g_x[:feat] + pltpu.roll(g_x[feat:], 1, 1)
        low = xd_ref[row_layer, r]
        high = jnp.where(r == rows - 1, rim_ref[...], xd_ref[row_layer, jnp.minimum(r + 1, rows - 1)])
        x_uv = jnp.concatenate((low[:feat], high[:feat]), 0)
        diff = high[feat:].astype(F32) - low[feat:].astype(F32)
        g_x, g_w, g_o = edges(planar, x_uv, diff, gates[2, pl.ds(r, 1), :])
        g_w_ref[0] += g_w
        g_o_ref[0] += g_o
        ns_ref[row_layer, r] += carry[...] + g_x[:feat]
        carry[...] = g_x[feat:]
        row_out(r).start()

    back_ref[...] = carry[...].astype(BF16)
    stores = copies(out_sems, (back_ref, back_hbm), (g_w_ref, g_w_hbm), (g_o_ref, g_o_hbm))
    for r in range(rows):
        row_out(r).wait()
    finish(stores)


def cross_kernel(r_ref, v0_ref, v1_ref, v2_ref, v3_ref, w_src_hbm, w_dst_hbm, w_out_hbm,
                 gw_hbm, go_hbm,
                 gu_hbm, gv0_hbm, gv1_hbm, gv2_hbm, gv3_hbm,
                 rf, vs, gvs, gate_rows, acc_w, acc_o, total,
                 w_src_ref, w_dst_ref, w_out_ref, gw_ref, go_ref, gu_ref, in_sems, out_sems):
    _, z, _ = place()
    loads = copies(
        in_sems,
        (w_src_hbm, w_src_ref), (w_dst_hbm, w_dst_ref), (w_out_hbm, w_out_ref),
        (gw_hbm, gw_ref), (go_hbm, go_ref),
    )
    zs = vs.shape[0]
    feat = vs.shape[2] // 2
    body = rf.shape[1]
    rf[...] = r_ref[:, :body, :].astype(F32)
    gate_rows[...] = jnp.sum(r_ref[:, body:, :].astype(F32), axis=0)
    for d, v_ref in enumerate((v0_ref, v1_ref, v2_ref, v3_ref)):
        vs[lax.rem(z + zs - d, zs)] = v_ref[...]
    acc_w[...] = jnp.zeros_like(acc_w)
    acc_o[...] = jnp.zeros_like(acc_o)
    finish(loads)
    via = load_weights(w_src_ref, w_dst_ref, w_out_ref, 1)

    @pl.loop(0, 8, unroll=2)
    def _(i):
        z2 = i // 4
        c2 = lax.rem(i, 4)
        us, vv, gg = [], [], []
        for zp in range(2):
            for cp in range(2):
                zt = z2 * 2 + zp
                cl = c2 * 2 + cp
                u = rf[:, pl.ds(zt * 64 + cl, 8, stride=8), :].reshape(128, 128).T
                us.append(u)
                vv.append(vs[zt, cl])
                gg.append(gate_rows[pl.ds(zt * 8 + cl, 1), :])
        u = jnp.concatenate(us, 1)
        v = jnp.concatenate(vv, 1)
        gate = jnp.concatenate(gg, 1)
        x_uv = jnp.concatenate((u[:feat].astype(BF16), v[:feat]), 0)
        g_x, g_w, g_o = edges(via, x_uv, v[feat:].astype(F32) - u[feat:], gate)
        acc_w[...] += g_w
        acc_o[...] += g_o
        turned = []
        for cp in range(2):
            lo, hi = cp * 128, (2 + cp) * 128
            gvs[z2 * 2, c2 * 2 + cp] = g_x[feat:, lo:lo + 128].astype(BF16)
            gvs[z2 * 2 + 1, c2 * 2 + cp] = g_x[feat:, hi:hi + 128].astype(BF16)
            both = jnp.concatenate((g_x[:feat, lo:lo + 128], g_x[:feat, hi:hi + 128]), 0)
            turned.append(both.T.reshape(16, 8, 128))
        at = pl.multiple_of(z2 * 64 + c2 * 16, 16)
        gu_ref[:, pl.ds(at, 16), :] = jnp.concatenate(turned, 1).astype(BF16)

    stores = copies(
        out_sems,
        *[
            (gvs.at[lax.rem(z + zs - d, zs)], gv_hbm)
            for d, gv_hbm in enumerate((gv0_hbm, gv1_hbm, gv2_hbm, gv3_hbm))
        ],
    )
    total[0:64] = gw_ref[0, :feat]
    total[64:128] = gw_ref[1, :feat] + acc_w[:feat]
    total[128:192] = gw_ref[0, feat:]
    total[192:256] = gw_ref[1, feat:] + acc_w[feat:]
    total[256:320] = go_ref[0]
    total[320:384] = go_ref[1] + acc_o[...]
    for k in range(16):
        piece = total[k * 24:k * 24 + 24]
        coarse = piece.astype(BF16).astype(F32)
        both = jnp.concatenate((coarse, piece - coarse), 0)
        gu_ref[k, 128:176, :] = both.astype(BF16)
    stores += copies(out_sems.at[4:], (gu_ref, gu_hbm))
    finish(stores)


def finish_kernel(gu_ref, gv0_ref, gv1_ref, gv2_ref, gv3_ref, back_ref, ns_hbm,
                  xd_hbm, usage_hbm, out_hbm,
                  guf, gvs, o0, o1, damps, ns_ref, xd_ref, usage_ref, out_ref,
                  in_sems, ns_sems, xd_sems, out_sems):
    pair, z, _ = place()
    loads = copies(in_sems, (usage_hbm, usage_ref))

    def rows_in(r):
        return (
            pltpu.make_async_copy(ns_hbm.at[:, r], ns_ref.at[:, r], ns_sems.at[r]),
            pltpu.make_async_copy(xd_hbm.at[:, r], xd_ref.at[:, r], xd_sems.at[r]),
        )

    for r in range(xd_ref.shape[1]):
        for copy in rows_in(r):
            copy.start()
    finish(loads)
    zs = gvs.shape[0]
    feat = xd_ref.shape[2] // 2
    rows = xd_ref.shape[1]
    row_layer = lax.rem(pair, 2)
    guf[...] = gu_ref[:, :128, :].astype(F32)
    for d, gv_ref in enumerate((gv0_ref, gv1_ref, gv2_ref, gv3_ref)):
        gvs[lax.rem(z + d, zs)] = gv_ref[...]
    damps[...] = lax.rsqrt(1.0 + usage_ref[0].astype(F32))

    @pl.loop(0, rows, unroll=2)
    def _(r):
        finish(rows_in(r))

        @pl.when(r == 0)
        def _():
            ns_ref[row_layer, 0] += back_ref[...].astype(F32)

        low, high = ns_ref[0, r], ns_ref[1, r]
        low = low + jnp.concatenate([gvs[q, r].astype(F32) for q in range(zs)], 1)
        parts = []
        for z2 in range(2):
            block = guf[:, pl.ds(z2 * 64 + r, 8, stride=8), :].reshape(128, 128).T
            parts += [block[:feat], block[feat:]]
        high = high + jnp.concatenate(parts, 1)
        low = xd_ref[0, r, feat:, :].astype(F32) + damps[0, pl.ds(r, 1), :] * low
        high = xd_ref[1, r, feat:, :].astype(F32) + damps[1, pl.ds(r, 1), :] * high
        spots = pl.ds(r, feat, stride=rows)
        for q in range(zs):
            o0[q, spots, :] = low[:, q * 128:(q + 1) * 128]
            o1[q, spots, :] = high[:, q * 128:(q + 1) * 128]

    stores = []
    for j, done in enumerate((o0, o1)):
        for q in range(zs):
            lanes = slice(q * 128, (q + 1) * 128)
            out_ref[j, :, :, lanes] = done[q].reshape(feat, rows, 128).astype(BF16)
        stores += copies(out_sems.at[j:], (out_ref.at[j], out_hbm.at[0, j]))
    finish(stores)


def shaped(*shape, dtype=F32):
    return pltpu.HBM(shape, dtype)


def all_to_all(value, axes):
    return lax.all_to_all(value, axes, 0, 0, tiled=True)


def call(kernel, out, scratch, *args, near=0):
    args = args[:near] + tuple(pltpu.with_memory_space_constraint(a, pltpu.HBM) for a in args[near:])
    return pl.pallas_call(
        kernel,
        out_shape=out,
        in_specs=[VMEM_SPEC] * near + [HBM_SPEC] * (len(args) - near),
        out_specs=jax.tree.map(lambda _: HBM_SPEC, out),
        scratch_shapes=scratch,
        compiler_params=PARAMS,
    )(*args)


def on_device(nodes, upstream, usage, blockage, capacity, w_src, w_dst, w_out):
    n_l, n_z, n_xy = lax.axis_size("l"), lax.axis_size("z"), lax.axis_size("xy")
    feat, rows, cols = nodes.shape[2:]
    axes = ("l", "z", "xy")

    def ident(l, k, i):
        return (l * n_z + k) * n_xy + i

    def cross_pairs(d):
        return [
            (ident(l + 1, k, i), ident(l, (k + d) % n_z, i))
            for l in range(n_l - 1) for k in range(n_z) for i in range(n_xy)
        ]

    strips = n_z * n_xy
    up = [(l * strips + s + 1, l * strips + s) for l in range(n_l) for s in range(strips - 1)]
    down = [(b, a) for a, b in up]

    xd, v0, v1, v2, v3, sent, rim = call(
        prepare_kernel,
        (
            shaped(2, rows, 2 * feat, cols, dtype=BF16),
            *[shaped(rows, 2 * feat, cols // n_z, dtype=BF16)] * 4,
            shaped(n_xy, 288, 2 * feat, dtype=BF16),
            shaped(2 * feat, cols, dtype=BF16),
        ),
        [
            VMEM((n_z, feat * rows, 128), F32), VMEM((n_z, feat * rows, 128), F32), VMEM((128, cols), F32),
            VMEM((2, feat, rows, cols), BF16), VMEM((2, feat, rows, cols), BF16),
            VMEM((2, rows, cols), jnp.int32), VMEM((rows, cols), jnp.int32), VMEM((rows, cols), jnp.int32),
            VMEM((2, rows, 2 * feat, cols), BF16), VMEM((n_z, rows, 2 * feat, 128), BF16),
            VMEM((n_xy, 288, 2 * feat), BF16), DMA((7,)), DMA((8,)),
        ],
        nodes, upstream, usage, blockage, capacity,
    )
    rim = lax.ppermute(rim, axes, up)
    got_u = all_to_all(sent, "xy")
    got_v = {d: lax.ppermute((v0, v1, v2, v3)[d], axes, cross_pairs(d)) for d in (2, 1, 3, 0)}
    got_v = [got_v[d] for d in range(4)]
    weights = (jnp.swapaxes(w_src, 1, 2), jnp.swapaxes(w_dst, 1, 2), w_out)
    held = [VMEM((2, feat, 128), BF16)] * 3
    ns, back, g_w, g_o = call(
        inside_kernel,
        (
            shaped(2, rows, feat, cols), shaped(feat, cols, dtype=BF16),
            shaped(2, 2 * feat, 128), shaped(2, feat, 128),
        ),
        [
            VMEM((3, rows, cols), F32), VMEM((feat, cols), F32), VMEM((2, rows, 2 * feat, cols), BF16),
            VMEM((1, 2, 2, rows, cols), jnp.int32), VMEM((1, 2, 2, rows, cols), jnp.int32), *held,
            VMEM((2, rows, feat, cols), F32), VMEM((feat, cols), BF16),
            VMEM((2, 2 * feat, 128), F32), VMEM((2, feat, 128), F32),
            DMA((5,)), DMA((rows,)), DMA((rows,)), DMA((3,)),
        ],
        rim, xd, blockage, capacity, *weights, near=1,
    )
    back = lax.ppermute(back, axes, down)
    gu, gv0, gv1, gv2, gv3 = call(
        cross_kernel,
        (
            shaped(n_xy, 176, 2 * feat, dtype=BF16),
            *[shaped(rows, feat, cols // n_z, dtype=BF16)] * 4,
        ),
        [
            VMEM((n_xy, 256, 128), F32), VMEM((n_z, rows, 2 * feat, 128), BF16),
            VMEM((n_z, rows, feat, 128), BF16), VMEM((32, 128), F32),
            VMEM((2 * feat, 128), F32), VMEM((feat, 128), F32), VMEM((384, 128), F32), *held,
            VMEM((2, 2 * feat, 128), F32), VMEM((2, feat, 128), F32),
            VMEM((n_xy, 176, 2 * feat), BF16), DMA((5,)), DMA((5,)),
        ],
        got_u, *got_v, *weights, g_w, g_o, near=5,
    )
    got_gu = all_to_all(gu, "xy")
    got_gv = [
        lax.ppermute(g, axes, [(b, a) for a, b in cross_pairs(d)])
        for d, g in enumerate((gv0, gv1, gv2, gv3))
    ]

    scale = 1.0 / math.sqrt(2 * n_l * cols * cols)
    part = got_gu[:, 128:, :].astype(F32).reshape(n_xy, 2, 24, 128)
    part = jnp.broadcast_to(jnp.sum(part, (0, 1))[None], (16, 24, 128))
    part = all_to_all(part, ("l", "z"))

    grad_nodes = call(
        finish_kernel,
        shaped(1, 2, feat, rows, cols, dtype=BF16),
        [
            VMEM((n_xy, 128, 128), F32), VMEM((n_z, rows, feat, 128), BF16),
            VMEM((n_z, feat * rows, 128), F32), VMEM((n_z, feat * rows, 128), F32),
            VMEM((2, rows, cols), F32), VMEM((2, rows, feat, cols), F32),
            VMEM((2, rows, 2 * feat, cols), BF16), VMEM((1, 2, rows, cols), jnp.int32),
            VMEM((2, feat, rows, cols), BF16), DMA((1,)), DMA((rows,)), DMA((rows,)), DMA((2,)),
        ],
        got_gu, *got_gv, back, ns, xd, usage, near=6,
    )
    part = jnp.broadcast_to(jnp.sum(part, 0)[None] * scale, (16, 24, 128))
    total = all_to_all(part, "xy").reshape(3, 2, feat, 128)
    return grad_nodes, jnp.swapaxes(total[0], 1, 2), jnp.swapaxes(total[1], 1, 2), total[2]


def solution(mesh):
    split = Mesh(mesh.devices.reshape(4, 4, 16), ("l", "z", "xy"))
    strip = ("z", "xy")
    placed = (
        P("l", None, None, strip, None),
        P("l", None, None, strip, None),
        P("l", None, strip, None),
        P("l", None, None, strip, None),
        P("l", None, None, strip, None),
        P(),
        P(),
        P(),
    )
    return jax.shard_map(
        on_device,
        mesh=split,
        in_specs=placed,
        out_specs=(P("l", None, None, strip, None), P(), P(), P()),
        check_vma=False,
    )
```

```python
import math

import jax
import jax.numpy as jnp
from jax import lax
from jax.experimental import pallas as pl
from jax.experimental.pallas import tpu as pltpu
from jax.sharding import Mesh, PartitionSpec as P


F32 = jnp.float32
BF16 = jnp.bfloat16
VMEM = pltpu.VMEM
VMEM_SPEC = pl.BlockSpec(memory_space=pltpu.VMEM)
HBM_SPEC = pl.BlockSpec(memory_space=pltpu.HBM)
DMA = pltpu.SemaphoreType.DMA
PARAMS = pltpu.CompilerParams(vmem_limit_bytes=24 * 1024 * 1024)


def copies(sems, *pairs):
    made = [pltpu.make_async_copy(a, b, sems.at[i]) for i, (a, b) in enumerate(pairs)]
    for copy in made:
        copy.start()
    return made


def finish(made):
    for copy in made:
        copy.wait()


def mm(a, b):
    return jnp.dot(a, b, preferred_element_type=F32)


def mm_nt(a, b):
    return lax.dot_general(a, b, (((1,), (1,)), ((), ())), preferred_element_type=F32)


def load_weights(w_src_ref, w_dst_ref, w_out_ref, t):
    w_cat_t = jnp.concatenate((w_src_ref[t].astype(F32), w_dst_ref[t].astype(F32)), 0)
    w_out_t = w_out_ref[t].astype(F32).T
    return w_cat_t.T.astype(BF16), w_cat_t.astype(BF16), w_out_t.astype(BF16)


def place():
    return lax.axis_index("l"), lax.axis_index("z"), lax.axis_index("xy")


def edges(weights, x_uv, diff, gate):
    w_cat, w_cat_t, w_out_t = weights
    pre = mm(w_cat, x_uv)
    sigma = 0.5 * jnp.tanh(0.5 * pre) + 0.5
    act = pre * sigma
    slope = sigma + act * (1.0 - sigma)
    g_msg = (gate * diff).astype(BF16)
    g_pre = (mm(w_out_t, g_msg) * slope).astype(BF16)
    g_w = mm_nt(x_uv, g_pre)
    g_o = mm_nt(g_msg, act.astype(BF16))
    g_x = mm(w_cat_t, g_pre)
    return g_x, g_w, g_o


def gate_of(blockage, capacity):
    return (1 - blockage).astype(F32) * capacity.astype(F32) * 0.25


def prepare_kernel(nodes_hbm, upstream_hbm, usage_hbm, block_hbm, cap_hbm,
                   xd_hbm, v0_hbm, v1_hbm, v2_hbm, v3_hbm, s_hbm, rim_hbm,
                   xs, ds, gs, nodes_ref, upstream_ref, usage_ref, block_ref, cap_ref,
                   xd_ref, v_ref, s_ref, in_sems, out_sems):
    pair, z, xy = place()
    feat, rows, cols = nodes_ref.shape[1:]
    zs = v_ref.shape[0]
    wide = cols // zs
    loads = copies(
        in_sems,
        (usage_hbm.at[0], usage_ref),
        (nodes_hbm.at[0, 0], nodes_ref.at[0]),
        (upstream_hbm.at[0, 0], upstream_ref.at[0]),
        (nodes_hbm.at[0, 1], nodes_ref.at[1]),
        (upstream_hbm.at[0, 1], upstream_ref.at[1]),
        (block_hbm.at[0, 1, 1], block_ref),
        (cap_hbm.at[0, 1, 1], cap_ref),
    )
    stores = []
    for j in range(2):
        finish(loads[:3] if j == 0 else loads[3:])
        damp = lax.rsqrt(1.0 + usage_ref[j].astype(F32))[None]
        scaled = (nodes_ref[j].astype(F32) * damp).reshape(feat * rows, cols)
        given = upstream_ref[j].astype(F32).reshape(feat * rows, cols)
        for q in range(zs):
            xs[q] = scaled[:, q * wide:(q + 1) * wide]
            ds[q] = given[:, q * wide:(q + 1) * wide]

        def row_of(r):
            at = pl.ds(r, feat, stride=rows)
            return jnp.concatenate(
                [jnp.concatenate((xs[q, at, :], ds[q, at, :]), 0) for q in range(zs)], 1
            )

        if j == 0:
            @pl.loop(0, rows, unroll=4)
            def _(r):
                xd_ref[0, r] = row_of(r).astype(BF16)
                for d in range(zs):
                    at = pl.multiple_of(lax.rem(z + d, zs) * wide, wide)
                    v_ref[d, r] = xd_ref[0, r, :, pl.ds(at, wide)]

            stores += copies(
                out_sems,
                (xd_ref.at[0], xd_hbm.at[0]),
                (v_ref.at[0], v0_hbm),
                (v_ref.at[1], v1_hbm),
                (v_ref.at[2], v2_hbm),
                (v_ref.at[3], v3_hbm),
            )
        else:
            @pl.loop(0, rows // 2, unroll=2)
            def _(half):
                pieces = []
                for k in range(2):
                    r = half * 2 + k
                    full = row_of(r)
                    xd_ref[1, r] = full.astype(BF16)
                    pieces.append([
                        full[:, q * wide:(q + 1) * wide].T.reshape(wide // 8, 8, 2 * feat)
                        for q in range(zs)
                    ])
                for q in range(zs):
                    both = jnp.concatenate((pieces[0][q], pieces[1][q]), 1)
                    at = pl.multiple_of(q * 8 * rows + half * 16, 16)
                    s_ref[:, pl.ds(at, 16), :] = both.astype(BF16)
    present = (pair < 3).astype(F32)
    gs[...] = jnp.zeros_like(gs)
    gs[pl.ds(pl.multiple_of(xy * 8, 8), 8), :] = gate_of(block_ref[...], cap_ref[...]) * present
    turned = [
        gs[:, q * wide:(q + 1) * wide].T.reshape(wide // 8, 8, wide) for q in range(zs)
    ]
    for q in range(0, zs, 2):
        both = jnp.concatenate((turned[q], turned[q + 1]), 1)
        s_ref[:, 8 * rows * zs + q * 8:8 * rows * zs + q * 8 + 16, :] = both.astype(BF16)
    stores += copies(
        out_sems.at[5:],
        (s_ref, s_hbm),
        (xd_ref.at[lax.rem(pair, 2), 0], rim_hbm),
        (xd_ref.at[1], xd_hbm.at[1]),
    )
    finish(stores)


def inside_kernel(rim_ref, xd_hbm, block_hbm, cap_hbm, w_src_hbm, w_dst_hbm, w_out_hbm,
                  ns_hbm, back_hbm, g_w_hbm, g_o_hbm,
                  gates, carry, xd_ref, block_ref, cap_ref, w_src_ref, w_dst_ref, w_out_ref,
                  ns_ref, back_ref, g_w_ref, g_o_ref, in_sems, row_sems, ns_sems, out_sems):
    pair, z, xy = place()
    loads = copies(
        in_sems,
        (block_hbm, block_ref), (cap_hbm, cap_ref),
        (w_src_hbm, w_src_ref), (w_dst_hbm, w_dst_ref), (w_out_hbm, w_out_ref),
    )

    def row_in(r):
        return pltpu.make_async_copy(xd_hbm.at[:, r], xd_ref.at[:, r], row_sems.at[r])

    def row_out(r):
        return pltpu.make_async_copy(ns_ref.at[:, r], ns_hbm.at[:, r], ns_sems.at[r])

    for r in range(xd_ref.shape[1]):
        row_in(r).start()
    finish(loads)
    feat = xd_ref.shape[2] // 2
    rows, cols = xd_ref.shape[1], xd_ref.shape[3]
    row_layer = lax.rem(pair, 2)
    col_layer = 1 - row_layer
    planar = load_weights(w_src_ref, w_dst_ref, w_out_ref, 0)
    via = load_weights(w_src_ref, w_dst_ref, w_out_ref, 1)
    last = lax.broadcasted_iota(jnp.int32, (rows, cols), 1) < cols - 1
    row_ids = (z * 16 + xy) * rows + lax.broadcasted_iota(jnp.int32, (rows, cols), 0)
    gates[0] = jnp.where(last, gate_of(block_ref[0, col_layer, 0], cap_ref[0, col_layer, 0]), 0.0)
    gates[1] = gate_of(block_ref[0, 0, 1], cap_ref[0, 0, 1])
    gates[2] = jnp.where(
        row_ids < cols - 1, gate_of(block_ref[0, row_layer, 0], cap_ref[0, row_layer, 0]), 0.0
    )
    g_w_ref[...] = jnp.zeros_like(g_w_ref)
    g_o_ref[...] = jnp.zeros_like(g_o_ref)
    carry[...] = jnp.zeros_like(carry)
    row_in(0).wait()

    @pl.loop(0, rows, unroll=2)
    def _(r):
        @pl.when(r + 1 < rows)
        def _():
            row_in(r + 1).wait()

        low, high = xd_ref[0, r], xd_ref[1, r]
        x_uv = jnp.concatenate((low[:feat], high[:feat]), 0)
        diff = high[feat:].astype(F32) - low[feat:].astype(F32)
        g_x, g_w, g_o = edges(via, x_uv, diff, gates[1, pl.ds(r, 1), :])
        g_w_ref[1] += g_w
        g_o_ref[1] += g_o
        ns_ref[0, r] = g_x[:feat]
        ns_ref[1, r] = g_x[feat:]
        own = xd_ref[col_layer, r].astype(F32)
        side = pltpu.roll(own, cols - 1, 1)
        x_col = jnp.concatenate((own[:feat], side[:feat]), 0).astype(BF16)
        low = xd_ref[row_layer, r]
        high = jnp.where(r == rows - 1, rim_ref[...], xd_ref[row_layer, jnp.minimum(r + 1, rows - 1)])
        x_row = jnp.concatenate((low[:feat], high[:feat]), 0)
        diff = high[feat:].astype(F32) - low[feat:].astype(F32)
        g_x, g_w, g_o = edges(
            planar,
            jnp.concatenate((x_col, x_row), 1),
            jnp.concatenate((side[feat:] - own[feat:], diff), 1),
            jnp.concatenate((gates[0, pl.ds(r, 1), :], gates[2, pl.ds(r, 1), :]), 1),
        )
        g_w_ref[0] += g_w
        g_o_ref[0] += g_o
        ns_ref[col_layer, r] += g_x[:feat, :cols] + pltpu.roll(g_x[feat:, :cols], 1, 1)
        ns_ref[row_layer, r] += carry[...] + g_x[:feat, cols:]
        carry[...] = g_x[feat:, cols:]
        row_out(r).start()

    back_ref[...] = carry[...].astype(BF16)
    stores = copies(out_sems, (back_ref, back_hbm), (g_w_ref, g_w_hbm), (g_o_ref, g_o_hbm))
    for r in range(rows):
        row_out(r).wait()
    finish(stores)


def cross_kernel(r_ref, v0_ref, v1_ref, v2_ref, v3_ref, w_src_hbm, w_dst_hbm, w_out_hbm,
                 gw_hbm, go_hbm,
                 gu_hbm, gv0_hbm, gv1_hbm, gv2_hbm, gv3_hbm,
                 rf, vs, gvs, gate_rows, acc_w, acc_o, total,
                 w_src_ref, w_dst_ref, w_out_ref, gw_ref, go_ref, gu_ref, in_sems, out_sems):
    _, z, _ = place()
    loads = copies(
        in_sems,
        (w_src_hbm, w_src_ref), (w_dst_hbm, w_dst_ref), (w_out_hbm, w_out_ref),
        (gw_hbm, gw_ref), (go_hbm, go_ref),
    )
    zs = vs.shape[0]
    feat = vs.shape[2] // 2
    body = rf.shape[1]
    rf[...] = r_ref[:, :body, :].astype(F32)
    gate_rows[...] = jnp.sum(r_ref[:, body:, :].astype(F32), axis=0)
    for d, v_ref in enumerate((v0_ref, v1_ref, v2_ref, v3_ref)):
        vs[lax.rem(z + zs - d, zs)] = v_ref[...]
    acc_w[...] = jnp.zeros_like(acc_w)
    acc_o[...] = jnp.zeros_like(acc_o)
    finish(loads)
    via = load_weights(w_src_ref, w_dst_ref, w_out_ref, 1)

    @pl.loop(0, 8, unroll=4)
    def _(i):
        z2 = i // 4
        c2 = lax.rem(i, 4)
        us, vv, gg = [], [], []
        for zp in range(2):
            for cp in range(2):
                zt = z2 * 2 + zp
                cl = c2 * 2 + cp
                u = rf[:, pl.ds(zt * 64 + cl, 8, stride=8), :].reshape(128, 128).T
                us.append(u)
                vv.append(vs[zt, cl])
                gg.append(gate_rows[pl.ds(zt * 8 + cl, 1), :])
        u = jnp.concatenate(us, 1)
        v = jnp.concatenate(vv, 1)
        gate = jnp.concatenate(gg, 1)
        x_uv = jnp.concatenate((u[:feat].astype(BF16), v[:feat]), 0)
        g_x, g_w, g_o = edges(via, x_uv, v[feat:].astype(F32) - u[feat:], gate)
        acc_w[...] += g_w
        acc_o[...] += g_o
        turned = []
        for cp in range(2):
            lo, hi = cp * 128, (2 + cp) * 128
            gvs[z2 * 2, c2 * 2 + cp] = g_x[feat:, lo:lo + 128].astype(BF16)
            gvs[z2 * 2 + 1, c2 * 2 + cp] = g_x[feat:, hi:hi + 128].astype(BF16)
            both = jnp.concatenate((g_x[:feat, lo:lo + 128], g_x[:feat, hi:hi + 128]), 0)
            turned.append(both.T.reshape(16, 8, 128))
        at = pl.multiple_of(z2 * 64 + c2 * 16, 16)
        gu_ref[:, pl.ds(at, 16), :] = jnp.concatenate(turned, 1).astype(BF16)

    stores = copies(
        out_sems,
        *[
            (gvs.at[lax.rem(z + zs - d, zs)], gv_hbm)
            for d, gv_hbm in enumerate((gv0_hbm, gv1_hbm, gv2_hbm, gv3_hbm))
        ],
    )
    total[0:64] = gw_ref[0, :feat]
    total[64:128] = gw_ref[1, :feat] + acc_w[:feat]
    total[128:192] = gw_ref[0, feat:]
    total[192:256] = gw_ref[1, feat:] + acc_w[feat:]
    total[256:320] = go_ref[0]
    total[320:384] = go_ref[1] + acc_o[...]
    for k in range(16):
        piece = total[k * 24:k * 24 + 24]
        coarse = piece.astype(BF16).astype(F32)
        both = jnp.concatenate((coarse, piece - coarse), 0)
        gu_ref[k, 128:176, :] = both.astype(BF16)
    stores += copies(out_sems.at[4:], (gu_ref, gu_hbm))
    finish(stores)


def finish_kernel(gu_ref, gv0_ref, gv1_ref, gv2_ref, gv3_ref, back_ref, ns_hbm,
                  xd_hbm, usage_hbm, out_hbm,
                  guf, gvs, o0, o1, damps, ns_ref, xd_ref, usage_ref, out_ref,
                  in_sems, ns_sems, xd_sems, out_sems):
    pair, z, _ = place()
    loads = copies(in_sems, (usage_hbm, usage_ref))

    def rows_in(r):
        return (
            pltpu.make_async_copy(ns_hbm.at[:, r], ns_ref.at[:, r], ns_sems.at[r]),
            pltpu.make_async_copy(xd_hbm.at[:, r], xd_ref.at[:, r], xd_sems.at[r]),
        )

    for r in range(xd_ref.shape[1]):
        for copy in rows_in(r):
            copy.start()
    finish(loads)
    zs = gvs.shape[0]
    feat = xd_ref.shape[2] // 2
    rows = xd_ref.shape[1]
    row_layer = lax.rem(pair, 2)
    guf[...] = gu_ref[:, :128, :].astype(F32)
    for d, gv_ref in enumerate((gv0_ref, gv1_ref, gv2_ref, gv3_ref)):
        gvs[lax.rem(z + d, zs)] = gv_ref[...]
    damps[...] = lax.rsqrt(1.0 + usage_ref[0].astype(F32))

    @pl.loop(0, rows, unroll=4)
    def _(r):
        finish(rows_in(r))

        @pl.when(r == 0)
        def _():
            ns_ref[row_layer, 0] += back_ref[...].astype(F32)

        low, high = ns_ref[0, r], ns_ref[1, r]
        low = low + jnp.concatenate([gvs[q, r].astype(F32) for q in range(zs)], 1)
        parts = []
        for z2 in range(2):
            block = guf[:, pl.ds(z2 * 64 + r, 8, stride=8), :].reshape(128, 128).T
            parts += [block[:feat], block[feat:]]
        high = high + jnp.concatenate(parts, 1)
        low = xd_ref[0, r, feat:, :].astype(F32) + damps[0, pl.ds(r, 1), :] * low
        high = xd_ref[1, r, feat:, :].astype(F32) + damps[1, pl.ds(r, 1), :] * high
        spots = pl.ds(r, feat, stride=rows)
        for q in range(zs):
            o0[q, spots, :] = low[:, q * 128:(q + 1) * 128]
            o1[q, spots, :] = high[:, q * 128:(q + 1) * 128]

    stores = []
    for j, done in enumerate((o0, o1)):
        for q in range(zs):
            lanes = slice(q * 128, (q + 1) * 128)
            out_ref[j, :, :, lanes] = done[q].reshape(feat, rows, 128).astype(BF16)
        stores += copies(out_sems.at[j:], (out_ref.at[j], out_hbm.at[0, j]))
    finish(stores)


def shaped(*shape, dtype=F32):
    return pltpu.HBM(shape, dtype)


def all_to_all(value, axes):
    return lax.all_to_all(value, axes, 0, 0, tiled=True)


def call(kernel, out, scratch, *args, near=0):
    args = args[:near] + tuple(pltpu.with_memory_space_constraint(a, pltpu.HBM) for a in args[near:])
    return pl.pallas_call(
        kernel,
        out_shape=out,
        in_specs=[VMEM_SPEC] * near + [HBM_SPEC] * (len(args) - near),
        out_specs=jax.tree.map(lambda _: HBM_SPEC, out),
        scratch_shapes=scratch,
        compiler_params=PARAMS,
    )(*args)


def on_device(nodes, upstream, usage, blockage, capacity, w_src, w_dst, w_out):
    n_l, n_z, n_xy = lax.axis_size("l"), lax.axis_size("z"), lax.axis_size("xy")
    feat, rows, cols = nodes.shape[2:]
    axes = ("l", "z", "xy")

    def ident(l, k, i):
        return (l * n_z + k) * n_xy + i

    def cross_pairs(d):
        return [
            (ident(l + 1, k, i), ident(l, (k + d) % n_z, i))
            for l in range(n_l - 1) for k in range(n_z) for i in range(n_xy)
        ]

    strips = n_z * n_xy
    up = [(l * strips + s + 1, l * strips + s) for l in range(n_l) for s in range(strips - 1)]
    down = [(b, a) for a, b in up]

    xd, v0, v1, v2, v3, sent, rim = call(
        prepare_kernel,
        (
            shaped(2, rows, 2 * feat, cols, dtype=BF16),
            *[shaped(rows, 2 * feat, cols // n_z, dtype=BF16)] * 4,
            shaped(n_xy, 288, 2 * feat, dtype=BF16),
            shaped(2 * feat, cols, dtype=BF16),
        ),
        [
            VMEM((n_z, feat * rows, 128), F32), VMEM((n_z, feat * rows, 128), F32), VMEM((128, cols), F32),
            VMEM((2, feat, rows, cols), BF16), VMEM((2, feat, rows, cols), BF16),
            VMEM((2, rows, cols), jnp.int32), VMEM((rows, cols), jnp.int32), VMEM((rows, cols), jnp.int32),
            VMEM((2, rows, 2 * feat, cols), BF16), VMEM((n_z, rows, 2 * feat, 128), BF16),
            VMEM((n_xy, 288, 2 * feat), BF16), DMA((7,)), DMA((8,)),
        ],
        nodes, upstream, usage, blockage, capacity,
    )
    rim = lax.ppermute(rim, axes, up)
    got_u = all_to_all(sent, "xy")
    got_v = {d: lax.ppermute((v0, v1, v2, v3)[d], axes, cross_pairs(d)) for d in (2, 1, 3, 0)}
    got_v = [got_v[d] for d in range(4)]
    weights = (jnp.swapaxes(w_src, 1, 2), jnp.swapaxes(w_dst, 1, 2), w_out)
    held = [VMEM((2, feat, 128), BF16)] * 3
    ns, back, g_w, g_o = call(
        inside_kernel,
        (
            shaped(2, rows, feat, cols), shaped(feat, cols, dtype=BF16),
            shaped(2, 2 * feat, 128), shaped(2, feat, 128),
        ),
        [
            VMEM((3, rows, cols), F32), VMEM((feat, cols), F32), VMEM((2, rows, 2 * feat, cols), BF16),
            VMEM((1, 2, 2, rows, cols), jnp.int32), VMEM((1, 2, 2, rows, cols), jnp.int32), *held,
            VMEM((2, rows, feat, cols), F32), VMEM((feat, cols), BF16),
            VMEM((2, 2 * feat, 128), F32), VMEM((2, feat, 128), F32),
            DMA((5,)), DMA((rows,)), DMA((rows,)), DMA((3,)),
        ],
        rim, xd, blockage, capacity, *weights, near=1,
    )
    back = lax.ppermute(back, axes, down)
    gu, gv0, gv1, gv2, gv3 = call(
        cross_kernel,
        (
            shaped(n_xy, 176, 2 * feat, dtype=BF16),
            *[shaped(rows, feat, cols // n_z, dtype=BF16)] * 4,
        ),
        [
            VMEM((n_xy, 256, 128), F32), VMEM((n_z, rows, 2 * feat, 128), BF16),
            VMEM((n_z, rows, feat, 128), BF16), VMEM((32, 128), F32),
            VMEM((2 * feat, 128), F32), VMEM((feat, 128), F32), VMEM((384, 128), F32), *held,
            VMEM((2, 2 * feat, 128), F32), VMEM((2, feat, 128), F32),
            VMEM((n_xy, 176, 2 * feat), BF16), DMA((5,)), DMA((5,)),
        ],
        got_u, *got_v, *weights, g_w, g_o, near=5,
    )
    got_gu = all_to_all(gu, "xy")
    got_gv = [
        lax.ppermute(g, axes, [(b, a) for a, b in cross_pairs(d)])
        for d, g in enumerate((gv0, gv1, gv2, gv3))
    ]

    scale = 1.0 / math.sqrt(2 * n_l * cols * cols)
    part = got_gu[:, 128:, :].astype(F32).reshape(n_xy, 2, 24, 128)
    part = jnp.broadcast_to(jnp.sum(part, (0, 1))[None], (16, 24, 128))
    part = all_to_all(part, ("l", "z"))
    part, got_gv[0] = lax.optimization_barrier((part, got_gv[0]))

    grad_nodes = call(
        finish_kernel,
        shaped(1, 2, feat, rows, cols, dtype=BF16),
        [
            VMEM((n_xy, 128, 128), F32), VMEM((n_z, rows, feat, 128), BF16),
            VMEM((n_z, feat * rows, 128), F32), VMEM((n_z, feat * rows, 128), F32),
            VMEM((2, rows, cols), F32), VMEM((2, rows, feat, cols), F32),
            VMEM((2, rows, 2 * feat, cols), BF16), VMEM((1, 2, rows, cols), jnp.int32),
            VMEM((2, feat, rows, cols), BF16), DMA((1,)), DMA((rows,)), DMA((rows,)), DMA((2,)),
        ],
        got_gu, *got_gv, back, ns, xd, usage, near=6,
    )
    part = jnp.broadcast_to(jnp.sum(part, 0)[None] * scale, (16, 24, 128))
    total = all_to_all(part, "xy").reshape(3, 2, feat, 128)
    return grad_nodes, jnp.swapaxes(total[0], 1, 2), jnp.swapaxes(total[1], 1, 2), total[2]


def solution(mesh):
    split = Mesh(mesh.devices.reshape(4, 4, 16), ("l", "z", "xy"))
    strip = ("z", "xy")
    placed = (
        P("l", None, None, strip, None),
        P("l", None, None, strip, None),
        P("l", None, strip, None),
        P("l", None, None, strip, None),
        P("l", None, None, strip, None),
        P(),
        P(),
        P(),
    )
    return jax.shard_map(
        on_device,
        mesh=split,
        in_specs=placed,
        out_specs=(P("l", None, None, strip, None), P(), P(), P()),
        check_vma=False,
    )
```
